32 devices in a mesh: leaf: 2 (over x), rows: 16 (over z, y, core).
Axes of the slice: x: 2, y: 2, z: 4, core: 2. Of those that a mesh axis runs over, the one named last changes fastest.
Arguments:
- features: bfloat16 [262144, 256], P(('leaf', 'rows')), parts along dimension 0, may hold values from -80 to 80
- node_ids: int32 [262144], P(('leaf', 'rows')), parts along dimension 0, may hold values from -1 to 15, as said below
- labels: int32 [262144], P(('leaf', 'rows')), parts along dimension 0, may hold values from 0 to 15
- owners: int32 [32], P('leaf'), parts along dimension 0, may hold values from 0 to 15, each once
Outputs:
- hyperplanes: float32 [32, 16, 256], P(('leaf', 'rows')), parts along dimension 0
- scores: float32 [16, 262144], P(None, ('leaf', 'rows')), parts along dimension 1
The draws below stay inside these ranges and needn't reach their ends.
There are 2 independent parts, one for each index of `leaf`. The reference program is written for one: setup_inputs(seed, part) draws one part's arguments, and reference() takes and returns one part's arrays. A program takes and returns all parts, laid end to end along the dimension named above; each array names one. Nothing has to cross between parts.
Inputs may be any that keep to these rules, and one draw needn't show every extreme that they name: `node_ids`: on rows device d, row p of node n's segment (local row n * 512 + p) holds n or -1; the live rows of a segment come first and there is at least one; some segment of every device is full. Each node number appears once in owners; node n is owned by the device of rows with index owners[n].
All inputs are finite; a program needn't handle non-finite values.
Results may differ from the reference program's by a relative error of at most 0.0035.
Values may be sent and summed in bfloat16 or wider, within the bound.
A program may use at most 128 MiB of HBM per device.

```python
import math
import jax
import jax.numpy as jnp
from jax import lax

F = 256
CLASSES = 16
ROW_DEV = 8192
NODES = 16
SEG = 512
TOTAL_ROWS = 131072
N_ROWS = 16


def label_draw(key):
    positions = jnp.arange(TOTAL_ROWS, dtype=jnp.int32)
    node_of = positions % ROW_DEV // SEG
    present = jax.random.randint(jax.random.fold_in(key, 11), (NODES, CLASSES), 0, 4) > 0
    forced = jnp.arange(CLASSES, dtype=jnp.int32)[None, :] == (jnp.arange(NODES, dtype=jnp.int32) % CLASSES)[:, None]
    present = (present | forced).astype(jnp.int32)
    noise = jax.random.randint(jax.random.fold_in(key, 12), (TOTAL_ROWS, CLASSES), 0, 1 << 20)
    ranked = noise + present[node_of] * (1 << 21)
    return jnp.argmax(ranked, axis=1).astype(jnp.int32)


def draw_labels(key, part):
    return label_draw(jax.random.fold_in(key, 5))


def draw_features(key, part):
    marks = label_draw(jax.random.fold_in(key, 5))
    base = jax.random.normal(jax.random.fold_in(key, 21), (TOTAL_ROWS, F), jnp.float32)
    mixing = jnp.eye(F, dtype=jnp.float32) + 0.5 * jax.random.normal(jax.random.fold_in(key, 22), (F, F), jnp.float32) / math.sqrt(F)
    centres = jax.random.normal(jax.random.fold_in(key, 23), (CLASSES, F), jnp.float32)
    values = jnp.dot(base, mixing, precision=lax.Precision.HIGHEST) + centres[marks]
    return jnp.clip(values, -80.0, 80.0).astype(jnp.bfloat16)


def draw_node_ids(key, part):
    device = jnp.arange(N_ROWS, dtype=jnp.int32)
    ceiling = jnp.maximum((SEG + 2 * SEG * device // max(N_ROWS - 1, 1)) // 3, 1)
    lengths = jax.random.randint(jax.random.fold_in(key, 31), (N_ROWS, NODES), 1, ceiling[:, None] + 1)
    filled = jnp.arange(NODES, dtype=jnp.int32)[None, :] == (device % NODES)[:, None]
    lengths = jnp.where(filled, SEG, lengths)
    within = jnp.arange(SEG, dtype=jnp.int32)
    node_index = jnp.broadcast_to(jnp.arange(NODES, dtype=jnp.int32)[None, :, None], (N_ROWS, NODES, SEG))
    result = jnp.where(within[None, None, :] < lengths[:, :, None], node_index, -1)
    return result.reshape(TOTAL_ROWS).astype(jnp.int32)


def setup_inputs(seed: int = 0, part: int = 0) -> dict:
    keys = jax.random.split(jax.random.key(seed), 5)
    own_keys = jax.random.split(jax.random.fold_in(keys[4], part), 5)
    return {
        "features": draw_features(jax.random.fold_in(jax.random.fold_in(keys[4], part), 71), part),
        "node_ids": draw_node_ids(jax.random.fold_in(jax.random.fold_in(keys[4], part), 71), part),
        "labels": draw_labels(jax.random.fold_in(jax.random.fold_in(keys[4], part), 71), part),
        "owners": jax.random.permutation(own_keys[3], NODES).astype(jnp.int32),
    }


ridge_term = 0.1

def solve_nodes(scatter, sums, counts):
    totals = jnp.sum(counts, axis=1)
    centers = jnp.sum(sums, axis=1) / totals[:, None]
    scaled = sums / jnp.maximum(counts, 1.0)[:, :, None]
    within = scatter - jnp.einsum('ncf,ncg->nfg', scaled, sums, precision=lax.Precision.HIGHEST)
    identity = jnp.eye(scatter.shape[-1], dtype=jnp.float32)
    system = within / totals[:, None, None] + ridge_term * identity
    shifts = (sums - counts[:, :, None] * centers[:, None, :]) / totals[:, None, None]
    factor = jnp.linalg.cholesky(system)
    planes = jax.vmap(lambda lower, right: jax.scipy.linalg.cho_solve((lower, True), right.T).T)(factor, shifts)
    offsets = -jnp.einsum('ncf,nf->nc', planes, centers, precision=lax.Precision.HIGHEST)
    return (planes, offsets)

def reference(features, node_ids, labels, owners):
    blocks = features.reshape(N_ROWS, NODES, SEG, F)
    live_rows = node_ids.reshape(N_ROWS, NODES, SEG) == jnp.arange(NODES, dtype=jnp.int32)[None, :, None]
    marks = labels.reshape(N_ROWS, NODES, SEG)
    classes = jnp.arange(CLASSES, dtype=jnp.int32)

    def one_node(index):
        chosen = lax.dynamic_index_in_dim(blocks, index, 1, keepdims=False)
        alive = lax.dynamic_index_in_dim(live_rows, index, 1, keepdims=False).reshape(-1)
        tags = lax.dynamic_index_in_dim(marks, index, 1, keepdims=False).reshape(-1)
        values = jnp.where(alive[:, None], chosen.reshape(-1, F).astype(jnp.float32), 0.0)
        onehot = ((tags[None, :] == classes[:, None]) & alive[None, :]).astype(jnp.float32)
        scatter = jnp.dot(values.T.astype(jnp.float32), values.astype(jnp.float32), preferred_element_type=jnp.float32, precision=lax.Precision.HIGHEST)
        sums = jnp.dot(onehot.astype(jnp.float32), values.astype(jnp.float32), preferred_element_type=jnp.float32, precision=lax.Precision.HIGHEST)
        counts = jnp.sum(onehot, axis=1)
        return (scatter, sums, counts)
    scatter, sums, counts = lax.map(one_node, jnp.arange(NODES, dtype=jnp.int32))
    planes, offsets = solve_nodes(scatter, sums, counts)
    inverse = jnp.zeros((NODES,), jnp.int32).at[owners].set(jnp.arange(NODES, dtype=jnp.int32))
    hyperplanes = jnp.take(planes, inverse, axis=0)
    rounded = lax.optimization_barrier(planes.astype(jnp.bfloat16)).astype(jnp.float32)

    def one_device(pair):
        chosen, alive = pair
        result = jnp.einsum('ncf,nsf->cns', rounded, chosen.astype(jnp.float32), precision=lax.Precision.HIGHEST)
        result = result + offsets.T[:, :, None]
        return jnp.where(alive[None], result, 0.0)
    scores = lax.map(one_device, (blocks, live_rows))
    scores = jnp.transpose(scores, (1, 0, 2, 3)).reshape(CLASSES, TOTAL_ROWS)
    return (hyperplanes, scores)
```

```python
import functools
import jax
import jax.numpy as jnp
from jax import lax
from jax.experimental import pallas as pl
from jax.experimental.pallas import tpu as pltpu
from jax.sharding import PartitionSpec as P

CLASSES = 16
LANES = 128
HALF = LANES // 2
GROUP = 8
RIDGE = 0.1
HIGHEST = lax.Precision.HIGHEST
NN = (((1,), (0,)), ((), ()))
TN = (((0,), (0,)), ((), ()))
NT = (((1,), (1,)), ((), ()))
TOP = HALF + 2 * CLASSES
EARLY = TOP + GROUP
LATE = LANES + HALF
SEND_EARLY, SEND_LATE, HOP, STEP = 1.3, 2.3, 2.0, 0.14
FIRST_EARLY, FIRST_LATE = 6.5, 12.0
VMEM = 67043328


def iota(shape, dim):
    return lax.broadcasted_iota(jnp.int32, shape, dim)


def partner_of(me, bit):
    width = 1 << bit
    return me + width * (1 - 2 * ((me // width) % 2))


def device_at(me, r):
    bit = 0
    while r >> bit:
        if (r >> bit) % 2:
            me = partner_of(me, bit)
        bit += 1
    return me


def exact(a, b, dims):
    return lax.dot_general(a, b, dims, precision=HIGHEST, preferred_element_type=jnp.float32)


def pack(square):
    top, low = square[:HALF, :], square[HALF:, :]
    turned = pltpu.roll(low, HALF, 1)
    row, col = iota((HALF, LANES), 0), iota((HALF, LANES), 1)
    packed = jnp.where((row >= col) | (col >= HALF), top, turned)
    diag = jnp.sum(jnp.where(row + HALF == col, low, 0.0), axis=0, keepdims=True)
    return packed, diag


def unpack(packed, diag):
    row, col = iota((HALF, LANES), 0), iota((HALF, LANES), 1)
    turned = jnp.concatenate([packed, jnp.zeros_like(packed)], axis=0).T
    top = jnp.where((row >= col) | (col >= HALF), packed, turned[:HALF, :])
    last = jnp.where(row < col, packed, jnp.where(row == col, diag, turned[:HALF, :]))
    low = jnp.where(col < HALF, turned[HALF:, :], pltpu.roll(last, HALF, 1))
    return jnp.concatenate([top, low], axis=0)


def one_partial(node, q, x_ref, ids_ref, labels_ref, early, late):
    seg, feat = x_ref.shape[1:]
    pieces = seg // LANES
    ids = ids_ref[pl.ds(node * pieces, pieces), :]
    tags = labels_ref[pl.ds(node * pieces, pieces), :]
    live = ids == node
    length = jnp.sum(live.astype(jnp.float32), axis=(0, 1), keepdims=True)
    x = x_ref[node]
    position = iota((seg, 1), 0).astype(jnp.float32)
    x = jnp.where(position < length, x, jnp.zeros((), x.dtype))
    tags = jnp.where(live, tags, -1)
    hot = jnp.concatenate(
        [tags[k : k + 1, :] == iota((CLASSES, LANES), 0) for k in range(pieces)], axis=1
    )
    hot = hot.astype(jnp.float32).astype(jnp.bfloat16)
    moment = lax.dot_general(x, x, TN, preferred_element_type=jnp.float32)
    sums = jnp.dot(hot, x, preferred_element_type=jnp.float32)
    counts = lax.dot_general(
        jnp.ones((GROUP, seg), jnp.bfloat16), hot, NT, preferred_element_type=jnp.float32
    )
    counts = jnp.concatenate([counts, jnp.zeros((GROUP, LANES - CLASSES), jnp.float32)], axis=1)
    packed, diag = pack(moment[:LANES, :LANES])
    early[q, 0:HALF, :] = packed
    early[q, HALF : HALF + CLASSES, :] = sums[:, :LANES]
    early[q, HALF + CLASSES : TOP, :] = sums[:, LANES:]
    packed, other = pack(moment[LANES:, LANES:])
    diag = diag + pltpu.roll(jnp.broadcast_to(other, (GROUP, LANES)), HALF, 1)
    early[q, TOP:EARLY, :] = jnp.where(iota((GROUP, LANES), 0) == 0, counts, diag)
    late[q, 0:LANES, :] = moment[:LANES, LANES:]
    late[q, LANES:LATE, :] = packed


def lane_of(x, lane):
    return jnp.broadcast_to(x[:, lane : lane + 1], x.shape)


def pivot(rows, at, whole):
    group, base = at // GROUP, at % GROUP
    lanes = iota((1, LANES), 1)
    pivots = rows[group]
    spread = [lane_of(pivots, at + u) for u in range(4)]
    d = [[spread[u][base + t : base + t + 1, :] for u in range(4)] for t in range(4)]
    a, b, c = d[0][0], d[0][1], d[1][1]
    inv = 1.0 / (a * c - b * b)
    p00, p01, p11 = c * inv, -b * inv, a * inv
    q00, q01, q10, q11 = d[0][2], d[0][3], d[1][2], d[1][3]
    t00, t01 = p00 * q00 + p01 * q10, p00 * q01 + p01 * q11
    t10, t11 = p01 * q00 + p11 * q10, p01 * q01 + p11 * q11
    s00 = d[2][2] - (q00 * t00 + q10 * t10)
    s01 = d[2][3] - (q00 * t01 + q10 * t11)
    s11 = d[3][3] - (q01 * t01 + q11 * t11)
    inv = 1.0 / (s00 * s11 - s01 * s01)
    h00, h01, h11 = s11 * inv, -s01 * inv, s00 * inv
    u00, u01 = t00 * h00 + t01 * h01, t00 * h01 + t01 * h11
    u10, u11 = t10 * h00 + t11 * h01, t10 * h01 + t11 * h11
    e00 = p00 + u00 * t00 + u01 * t01
    e01 = p01 + u00 * t10 + u01 * t11
    e11 = p11 + u10 * t10 + u11 * t11
    dinv = [
        [e00, e01, -u00, -u01],
        [e01, e11, -u10, -u11],
        [-u00, -u10, h00, h01],
        [-u01, -u11, h01, h11],
    ]
    inside = (lanes >= at) & (lanes < at + 4)
    near = [
        jnp.where(inside, jnp.where(lanes == at + t, -1.0, 0.0), pivots[base + t : base + t + 1, :])
        for t in range(4)
    ]
    mix = lambda t: (dinv[t][0] * near[0] + dinv[t][1] * near[1]) + (
        dinv[t][2] * near[2] + dinv[t][3] * near[3]
    )
    w = [jnp.broadcast_to(mix(t), (GROUP, LANES)) for t in range(4)]
    inside = jnp.broadcast_to(inside, (GROUP, LANES))
    depth = iota((GROUP, LANES), 0)
    out = list(rows)
    first = 0 if whole else (group if base == 0 else group + 1)
    for g in range(first, len(rows)):
        x = rows[g]
        k = [lane_of(x, at + u) for u in range(4)]
        gone = inside
        if whole and g == group:
            own = (depth >= base) & (depth < base + 4)
            k = [jnp.where(own, jnp.where(depth == base + u, 1.0, 0.0), k[u]) for u in range(4)]
            gone = inside | own
        x = jnp.where(gone, 0.0, x)
        out[g] = x - ((k[0] * w[0] + k[1] * w[1]) + (k[2] * w[2] + k[3] * w[3]))
    return out


def rows_of(x):
    return [x[g : g + GROUP, :] for g in range(0, x.shape[0], GROUP)]


def tree_kernel(
    n,
    owners_hbm,
    x_hbm,
    ids_hbm,
    labels_hbm,
    planes_ref,
    out_ref,
    owners_ref,
    nodes_ref,
    x_ref,
    ids_ref,
    labels_ref,
    early,
    early_in,
    late,
    late_in,
    mine,
    messages,
    scores,
    load_sems,
    early_send,
    early_recv,
    late_send,
    late_recv,
    far_send,
    far_recv,
    near_send,
    near_recv,
):
    bits = n.bit_length() - 1
    seg, feat = x_ref.shape[1:]
    pieces = seg // LANES
    me = lax.axis_index("rows")
    barrier = pltpu.get_barrier_semaphore()
    pairs = [(owners_hbm, owners_ref), (ids_hbm, ids_ref), (labels_hbm, labels_ref), (x_hbm, x_ref)]
    loads = [pltpu.make_async_copy(a, b, load_sems.at[k]) for k, (a, b) in enumerate(pairs)]
    for load in loads:
        load.start()
    for bit in range(bits):
        pl.semaphore_signal(barrier, inc=1, device_id={"rows": partner_of(me, bit)})
    for load in loads:
        load.wait()
    pl.semaphore_wait(barrier, bits)

    def copy_of(part, step, q):
        held, landed, send, recv = (
            (early, early_in, early_send, early_recv),
            (late, late_in, late_send, late_recv),
        )[part]
        return pltpu.make_async_remote_copy(
            src_ref=held.at[q],
            dst_ref=landed.at[q],
            send_sem=send.at[q],
            recv_sem=recv.at[q],
            device_id={"rows": partner_of(me, step)},
        )

    def partial(q):
        slot = 0
        for b in range(bits):
            mine, theirs = (me // (1 << b)) % 2, (q // (1 << (bits - 1 - b))) % 2
            slot = slot + (1 << b) * ((mine + theirs) % 2)
        node = 0
        for k in range(n):
            node = jnp.where(owners_ref[k] == slot, k, node)
        nodes_ref[q] = node
        one_partial(node, q, x_ref, ids_ref, labels_ref, early, late)

    def finish(part, step, q):
        half = n >> (step + 1)
        copy_of(part, step, q + half).wait_recv()
        held, landed = (early, early_in) if part == 0 else (late, late_in)
        held[q] = held[q] + landed[q + half]

    quarter = n // 4

    def turn(i):
        low = quarter - 1 - i % quarter
        for b in range(bits - 2):
            yield (low // (1 << b)) % 2, bits - 3 - b
        yield 1 - i // quarter, bits - 2

    def block_at(i):
        return sum(bit * (1 << place) for bit, place in turn(i))

    def pair(i, carry):
        q = block_at(i)
        partial(q + n // 2)
        copy_of(0, 0, q + n // 2).start()
        copy_of(1, 0, q + n // 2).start()
        partial(q)

        @pl.when(i >= 1)
        def _():
            before = block_at(i - 1)
            finish(0, 0, before)

            @pl.when(i - 1 < quarter)
            def _():
                copy_of(0, 1, before).start()

            finish(1, 0, before)

        @pl.when(i >= quarter + 1)
        def _():
            copy_of(1, 1, block_at(i - 1 - quarter)).start()

        @pl.when(i >= quarter + 2)
        def _():
            before = block_at(i - 2)
            finish(0, 1, before)

            @pl.when(before >= n // 8)
            def _():
                copy_of(0, 2, before).start()

        return carry

    lax.fori_loop(0, n // 2, pair, 0)
    finish(0, 0, 0)
    copy_of(1, 1, block_at(quarter - 1)).start()
    finish(1, 0, 0)

    def times(first, gap):
        when = {(1, block_at(quarter + j)): first + gap * j for j in range(quarter)}
        for step in range(2, bits):
            half = n >> (step + 1)
            for q in range(half):
                when[step, q] = max(when[step - 1, q], when[step - 1, q + half] + HOP + gap)
        return when

    done = {block_at(i) for i in range(quarter, n // 2 - 2)}
    first = times(FIRST_EARLY, SEND_EARLY)
    last = times(FIRST_LATE, SEND_LATE)
    events = [(at, step, 0, q) for (step, q), at in first.items() if step > 1 or q not in done]
    events = sorted(events + [(at, step, 1, q) for (step, q), at in last.items()])
    begin = first[bits - 1, 0]

    def advance(part, step, q):
        finish(part, step, q)
        if step < bits - 1 and q >= n >> (step + 2):
            copy_of(part, step + 1, q).start()

    while events and events[0][0] <= begin:
        at, step, part, q = events.pop(0)
        advance(part, step, q)

    sums = jnp.concatenate(
        [early[0, HALF : HALF + CLASSES, :], early[0, HALF + CLASSES : TOP, :]], axis=1
    )
    count_row = early[0, TOP : TOP + 1, 0:CLASSES]
    eye = iota((CLASSES, CLASSES), 0) == iota((CLASSES, CLASSES), 1)
    counts = jnp.sum(jnp.where(eye, count_row, 0.0), axis=1, keepdims=True)
    total = jnp.sum(counts, axis=0, keepdims=True)
    centers = jnp.sum(sums, axis=0, keepdims=True) / total
    scaled = sums / jnp.maximum(counts, 1.0)
    row, col = iota((LANES, LANES), 0), iota((LANES, LANES), 1)
    ridge = jnp.where(row == col, RIDGE, 0.0)
    diag = early[0, TOP + 1 : TOP + 2, :]
    between = exact(scaled, sums, TN)
    shifts = (sums - counts * centers) / total
    square = unpack(early[0, 0:HALF, :], pltpu.roll(jnp.broadcast_to(diag, (GROUP, LANES)), HALF, 1)[0:1, :])
    rows = rows_of((square - between[:LANES, :LANES]) / total + ridge)
    for turned in range(LANES // 4):
        while events and events[0][0] <= begin + STEP * turned:
            at, step, part, q = events.pop(0)
            advance(part, step, q)
        rows = pivot(rows, 4 * turned, True)
    for at, step, part, q in events:
        advance(part, step, q)

    inverse = jnp.concatenate(rows, axis=0)
    cross = (late[0, 0:LANES, :] - between[:LANES, LANES:]) / total
    square = unpack(late[0, LANES:LATE, :], diag)
    last = (square - between[LANES:, LANES:]) / total + ridge
    gain = exact(inverse, cross, NN)
    schur = last - exact(cross, gain, TN)
    right = shifts[:, LANES:] - exact(shifts[:, :LANES], gain, NN)
    left = exact(shifts[:, :LANES], inverse, NN)
    rows = rows_of(schur) + rows_of(right)
    for step in range(LANES // 4):
        rows = pivot(rows, 4 * step, False)
    right = jnp.concatenate(rows[LANES // GROUP :], axis=0)
    left = left - exact(right, gain, NT)
    planes = jnp.concatenate([left, right], axis=1)
    planes_ref[...] = planes
    offsets = -jnp.sum(planes * centers, axis=1, keepdims=True)
    high = offsets.astype(jnp.bfloat16).astype(jnp.float32)
    middle = (offsets - high).astype(jnp.bfloat16).astype(jnp.float32)
    low = offsets - high - middle
    lane = iota((CLASSES, LANES), 1)
    third = LANES // 4
    coded = jnp.where(lane < third, high, jnp.where(lane < 2 * third, middle, low))
    mine[:, 0:feat] = planes.astype(jnp.bfloat16)
    mine[:, feat : feat + LANES] = coded.astype(jnp.bfloat16)

    def far_copy(r):
        return pltpu.make_async_remote_copy(
            src_ref=mine,
            dst_ref=messages.at[r],
            send_sem=far_send.at[r // 2],
            recv_sem=far_recv.at[r // 2],
            device_id={"rows": device_at(me, r)},
        )

    def near_copy(r):
        return pltpu.make_async_remote_copy(
            src_ref=mine if r == 0 else messages.at[r],
            dst_ref=messages.at[r + 1],
            send_sem=near_send.at[r // 2],
            recv_sem=near_recv.at[r // 2],
            device_id={"rows": partner_of(me, 0)},
        )

    def score(r):
        q = sum(((r >> b) % 2) << (bits - 1 - b) for b in range(bits))
        node = nodes_ref[q]
        message = mine if r == 0 else messages.at[r]
        coded = message[:, feat : feat + LANES].astype(jnp.float32)
        offsets = coded[:, 0:1] + coded[:, third : third + 1] + coded[:, 2 * third : 2 * third + 1]
        values = lax.dot_general(
            message[:, 0:feat], x_ref[node], NT, preferred_element_type=jnp.float32
        )
        values = values + offsets
        ids = ids_ref[pl.ds(node * pieces, pieces), :]
        for k in range(pieces):
            part = values[:, k * LANES : (k + 1) * LANES]
            scores[r, :, k * LANES : (k + 1) * LANES] = jnp.where(ids[k : k + 1, :] == node, part, 0.0)

    turns = list(range(2, n, 2))
    for r in reversed(turns):
        far_copy(r).start()
    near_copy(0).start()
    score(0)
    for r in turns:
        far_copy(r).wait_recv()
        near_copy(r).start()
        near_copy(r - 2).wait_recv()
        score(r - 1)
        score(r)
    near_copy(n - 2).wait_recv()
    score(n - 1)
    for k in range(n):
        out_ref[:, k * seg : (k + 1) * seg] = scores[lax.bitwise_xor(owners_ref[k], me)]
    for part, send in ((0, early_send), (1, late_send)):
        for step in range(bits):
            half = n >> (step + 1)
            for q in range(half, 2 * half):
                copy_of(part, step, q).wait_send()
    for r in turns:
        far_copy(r).wait_send()
    for r in range(0, n, 2):
        near_copy(r).wait_send()


def on_device(features, node_ids, labels, owners):
    row_count, feat = features.shape
    n = owners.shape[0]
    seg = row_count // n
    ids = node_ids.reshape(row_count // LANES, LANES)
    tags = labels.reshape(row_count // LANES, LANES)
    hbm = pl.BlockSpec(memory_space=pltpu.HBM)
    whole = pl.BlockSpec(memory_space=pltpu.VMEM)
    dma = pltpu.SemaphoreType.DMA

    planes, scores = pl.pallas_call(
        functools.partial(tree_kernel, n),
        out_shape=(
            pltpu.VMEM((CLASSES, feat), jnp.float32),
            pltpu.VMEM((CLASSES, row_count), jnp.float32),
        ),
        in_specs=[hbm] * 4,
        out_specs=(whole, whole),
        scratch_shapes=[
            pltpu.SMEM((n,), jnp.int32),
            pltpu.SMEM((n,), jnp.int32),
            pltpu.VMEM((n, seg, feat), features.dtype),
            pltpu.VMEM(ids.shape, jnp.int32),
            pltpu.VMEM(ids.shape, jnp.int32),
            pltpu.VMEM((n, EARLY, LANES), jnp.float32),
            pltpu.VMEM((n, EARLY, LANES), jnp.float32),
            pltpu.VMEM((n, LATE, LANES), jnp.float32),
            pltpu.VMEM((n, LATE, LANES), jnp.float32),
            pltpu.VMEM((CLASSES, feat + LANES), jnp.bfloat16),
            pltpu.VMEM((n, CLASSES, feat + LANES), jnp.bfloat16),
            pltpu.VMEM((n, CLASSES, seg), jnp.float32),
            dma((4,)),
            dma((n,)),
            dma((n,)),
            dma((n,)),
            dma((n,)),
            dma((n // 2,)),
            dma((n // 2,)),
            dma((n // 2,)),
            dma((n // 2,)),
        ],
        compiler_params=pltpu.CompilerParams(
            collective_id=0, has_side_effects=True, vmem_limit_bytes=VMEM - 4 * CLASSES * (row_count + feat)
        ),
        name="tree",
    )(owners, features.reshape(n, seg, feat), ids, tags)

    return planes[None], scores


def solution(mesh):
    in_specs = (P(("leaf", "rows"), None), P(("leaf", "rows")), P(("leaf", "rows")), P("leaf"))
    out_specs = (P(("leaf", "rows"), None, None), P(None, ("leaf", "rows")))
    return jax.shard_map(
        on_device, mesh=mesh, in_specs=in_specs, out_specs=out_specs, check_vma=False
    )
```

```python
import functools
import jax
import jax.numpy as jnp
from jax import lax
from jax.experimental import pallas as pl
from jax.experimental.pallas import tpu as pltpu
from jax.sharding import PartitionSpec as P

CLASSES = 16
LANES = 128
HALF = LANES // 2
GROUP = 8
WIDTH = 4
RIDGE = 0.1
HIGHEST = lax.Precision.HIGHEST
NN = (((1,), (0,)), ((), ()))
TN = (((0,), (0,)), ((), ()))
NT = (((1,), (1,)), ((), ()))
TOP = HALF + 2 * CLASSES
EARLY = TOP + GROUP
LATE = LANES + HALF
EARLY_CUTS = (0, EARLY)
LATE_CUTS = (0, 96, LATE)
RATE, NEAR, FAR, STEP = 0.012, 1.8, 2.6, 0.16
OPEN, TURN = 4.0, 0.7
VMEM = 67043328


def iota(shape, dim):
    return lax.broadcasted_iota(jnp.int32, shape, dim)


def partner_of(me, bit):
    width = 1 << bit
    return me + width * (1 - 2 * ((me // width) % 2))


def device_at(me, r):
    bit = 0
    while r >> bit:
        if (r >> bit) % 2:
            me = partner_of(me, bit)
        bit += 1
    return me


def exact(a, b, dims):
    return lax.dot_general(a, b, dims, precision=HIGHEST, preferred_element_type=jnp.float32)


def pack(square):
    top, low = square[:HALF, :], square[HALF:, :]
    turned = pltpu.roll(low, HALF, 1)
    row, col = iota((HALF, LANES), 0), iota((HALF, LANES), 1)
    packed = jnp.where((row >= col) | (col >= HALF), top, turned)
    diag = jnp.sum(jnp.where(row + HALF == col, low, 0.0), axis=0, keepdims=True)
    return packed, diag


def unpack(packed, diag):
    row, col = iota((HALF, LANES), 0), iota((HALF, LANES), 1)
    turned = jnp.concatenate([packed, jnp.zeros_like(packed)], axis=0).T
    top = jnp.where((row >= col) | (col >= HALF), packed, turned[:HALF, :])
    last = jnp.where(row < col, packed, jnp.where(row == col, diag, turned[:HALF, :]))
    low = jnp.where(col < HALF, turned[HALF:, :], pltpu.roll(last, HALF, 1))
    return jnp.concatenate([top, low], axis=0)


def mark(node, ids_ref, labels_ref, hot_ref, tally_ref):
    seg = hot_ref.shape[2]
    tiles = seg // LANES
    tags = labels_ref[pl.ds(node * tiles, tiles), :]
    live = ids_ref[pl.ds(node * tiles, tiles), :] == node
    length = jnp.sum(live.astype(jnp.float32), axis=(0, 1), keepdims=True)
    tags = jnp.where(live, tags, -1)
    hot = jnp.concatenate(
        [tags[k : k + 1, :] == iota((CLASSES, LANES), 0) for k in range(tiles)], axis=1
    )
    hot = hot.astype(jnp.float32).astype(jnp.bfloat16)
    counts = lax.dot_general(
        jnp.ones((GROUP, seg), jnp.bfloat16), hot, NT, preferred_element_type=jnp.float32
    )
    counts = jnp.concatenate([counts, jnp.zeros((GROUP, LANES - CLASSES), jnp.float32)], axis=1)
    hot_ref[node] = hot
    tally_ref[node] = jnp.where(iota((GROUP, LANES), 0) == 0, counts, length)


def one_partial(node, q, x_ref, hot_ref, tally_ref, early, late):
    seg, feat = x_ref.shape[1:]
    tally = tally_ref[node]
    x = x_ref[node]
    position = iota((seg, feat), 0).astype(jnp.float32)
    length = jnp.concatenate([tally[1:2, :]] * (feat // LANES), axis=1)
    x = jnp.where(position < length, x, jnp.zeros((), x.dtype))
    moment = lax.dot_general(x, x, TN, preferred_element_type=jnp.float32)
    sums = jnp.dot(hot_ref[node], x, preferred_element_type=jnp.float32)
    packed, diag = pack(moment[:LANES, :LANES])
    early[q, 0:HALF, :] = packed
    early[q, HALF : HALF + CLASSES, :] = sums[:, :LANES]
    early[q, HALF + CLASSES : TOP, :] = sums[:, LANES:]
    packed, other = pack(moment[LANES:, LANES:])
    diag = diag + pltpu.roll(jnp.broadcast_to(other, (GROUP, LANES)), HALF, 1)
    early[q, TOP:EARLY, :] = jnp.where(iota((GROUP, LANES), 0) == 0, tally, diag)
    late[q, 0:LANES, :] = moment[:LANES, LANES:]
    late[q, LANES:LATE, :] = packed


def lane_of(x, lane):
    return jnp.broadcast_to(x[:, lane : lane + 1], x.shape)


def pivot(rows, at, whole):
    group, base = at // GROUP, at % GROUP
    lanes = iota((1, LANES), 1)
    pivots = rows[group]
    spread = [lane_of(pivots, at + u) for u in range(4)]
    d = [[spread[u][base + t : base + t + 1, :] for u in range(4)] for t in range(4)]
    a, b, c = d[0][0], d[0][1], d[1][1]
    inv = 1.0 / (a * c - b * b)
    p00, p01, p11 = c * inv, -b * inv, a * inv
    q00, q01, q10, q11 = d[0][2], d[0][3], d[1][2], d[1][3]
    t00, t01 = p00 * q00 + p01 * q10, p00 * q01 + p01 * q11
    t10, t11 = p01 * q00 + p11 * q10, p01 * q01 + p11 * q11
    s00 = d[2][2] - (q00 * t00 + q10 * t10)
    s01 = d[2][3] - (q00 * t01 + q10 * t11)
    s11 = d[3][3] - (q01 * t01 + q11 * t11)
    inv = 1.0 / (s00 * s11 - s01 * s01)
    h00, h01, h11 = s11 * inv, -s01 * inv, s00 * inv
    u00, u01 = t00 * h00 + t01 * h01, t00 * h01 + t01 * h11
    u10, u11 = t10 * h00 + t11 * h01, t10 * h01 + t11 * h11
    e00 = p00 + u00 * t00 + u01 * t01
    e01 = p01 + u00 * t10 + u01 * t11
    e11 = p11 + u10 * t10 + u11 * t11
    dinv = [
        [e00, e01, -u00, -u01],
        [e01, e11, -u10, -u11],
        [-u00, -u10, h00, h01],
        [-u01, -u11, h01, h11],
    ]
    inside = (lanes >= at) & (lanes < at + 4)
    near = [
        jnp.where(inside, jnp.where(lanes == at + t, -1.0, 0.0), pivots[base + t : base + t + 1, :])
        for t in range(4)
    ]
    mix = lambda t: (dinv[t][0] * near[0] + dinv[t][1] * near[1]) + (
        dinv[t][2] * near[2] + dinv[t][3] * near[3]
    )
    w = [jnp.broadcast_to(mix(t), (GROUP, LANES)) for t in range(4)]
    inside = jnp.broadcast_to(inside, (GROUP, LANES))
    depth = iota((GROUP, LANES), 0)
    out = list(rows)
    first = 0 if whole else (group if base == 0 else group + 1)
    for g in range(first, len(rows)):
        x = rows[g]
        k = [lane_of(x, at + u) for u in range(4)]
        gone = inside
        if whole and g == group:
            own = (depth >= base) & (depth < base + 4)
            k = [jnp.where(own, jnp.where(depth == base + u, 1.0, 0.0), k[u]) for u in range(4)]
            gone = inside | own
        x = jnp.where(gone, 0.0, x)
        out[g] = x - ((k[0] * w[0] + k[1] * w[1]) + (k[2] * w[2] + k[3] * w[3]))
    return out


def rows_of(x):
    return [x[g : g + GROUP, :] for g in range(0, x.shape[0], GROUP)]


def tree_kernel(
    n,
    owners_hbm,
    x_hbm,
    ids_hbm,
    labels_hbm,
    planes_ref,
    out_ref,
    owners_ref,
    nodes_ref,
    x_ref,
    ids_ref,
    labels_ref,
    hot_ref,
    tally_ref,
    early,
    early_in,
    late,
    late_in,
    mine,
    messages,
    mine_offsets,
    message_offsets,
    scores,
    load_sems,
    sum_send,
    sum_recv,
    far_send,
    far_recv,
    near_send,
    near_recv,
):
    bits = n.bit_length() - 1
    seg, feat = x_ref.shape[1:]
    tiles = seg // LANES
    me = lax.axis_index("rows")
    barrier = pltpu.get_barrier_semaphore()
    pairs = [(owners_hbm, owners_ref), (ids_hbm, ids_ref), (labels_hbm, labels_ref), (x_hbm, x_ref)]
    loads = [pltpu.make_async_copy(a, b, load_sems.at[k]) for k, (a, b) in enumerate(pairs)]
    for load in loads:
        load.start()
    for bit in range(bits):
        pl.semaphore_signal(barrier, inc=1, device_id={"rows": partner_of(me, bit)})
    for load in loads[:-1]:
        load.wait()

    def prepare(k, carry):
        mark(k, ids_ref, labels_ref, hot_ref, tally_ref)
        return carry

    lax.fori_loop(0, n, prepare, 0, unroll=8)
    loads[-1].wait()
    pl.semaphore_wait(barrier, bits)

    wholes = [(0, 0, EARLY, 0), (1, 0, LATE, 1)]
    pieces = list(wholes)
    for part, cuts in enumerate((EARLY_CUTS, LATE_CUTS)):
        pieces += [(part, lo, hi - lo, len(pieces) + k) for k, (lo, hi) in enumerate(zip(cuts, cuts[1:]))]
    firsts, lasts = ([p for p in pieces[2:] if p[0] == part] for part in (0, 1))
    held, landed = (early, late), (early_in, late_in)

    def copy_of(piece, step, q):
        part, low, size, sem = piece
        return pltpu.make_async_remote_copy(
            src_ref=held[part].at[q, pl.ds(low, size)],
            dst_ref=landed[part].at[q, pl.ds(low, size)],
            send_sem=sum_send.at[sem, q],
            recv_sem=sum_recv.at[sem, q],
            device_id={"rows": partner_of(me, step)},
        )

    def partial(q):
        slot = 0
        for b in range(bits):
            mine, theirs = (me // (1 << b)) % 2, (q // (1 << (bits - 1 - b))) % 2
            slot = slot + (1 << b) * ((mine + theirs) % 2)
        node = 0
        for k in range(n):
            node = jnp.where(owners_ref[k] == slot, k, node)
        nodes_ref[q] = node
        one_partial(node, q, x_ref, hot_ref, tally_ref, early, late)

    def finish(piece, step, q):
        half = n >> (step + 1)
        copy_of(piece, step, q + half).wait_recv()
        part, low, size, sem = piece
        rows = pl.ds(low, size)
        held[part][q, rows] = held[part][q, rows] + landed[part][q + half, rows]

    quarter = n // 4

    def turn(i):
        low = quarter - 1 - i % quarter
        for b in range(bits - 2):
            yield (low // (1 << b)) % 2, bits - 3 - b
        yield 1 - i // quarter, bits - 2

    def block_at(i):
        return sum(bit * (1 << place) for bit, place in turn(i))

    def pair(i, carry):
        q = block_at(i)
        partial(q + n // 2)
        partial(q)
        for piece in wholes:
            copy_of(piece, 0, q + n // 2).start()

        @pl.when(i >= 1)
        def _():
            before = block_at(i - 1)
            finish(wholes[0], 0, before)

            @pl.when(i - 1 < quarter)
            def _():
                for piece in firsts:
                    copy_of(piece, 1, before).start()

            finish(wholes[1], 0, before)

        @pl.when(i >= quarter + 1)
        def _():
            for piece in lasts:
                copy_of(piece, 1, block_at(i - 1 - quarter)).start()

        @pl.when(i >= quarter + 2)
        def _():
            before = block_at(i - 2)
            for piece in firsts:
                finish(piece, 1, before)

            @pl.when(before >= n // 8)
            def _():
                for piece in firsts:
                    copy_of(piece, 2, before).start()

        return carry

    lax.fori_loop(0, n // 2, pair, 0)
    finish(wholes[0], 0, 0)
    for piece in lasts:
        copy_of(piece, 1, block_at(quarter - 1)).start()
    finish(wholes[1], 0, 0)

    free = [0.0] * bits
    queue = []

    def post(at, step, q, piece):
        begin = max(at, free[step])
        free[step] = begin + RATE * piece[2]
        queue.append((free[step] + (NEAR if step < bits - 1 else FAR), step, piece[3], q - (n >> (step + 1))))

    for part, group in enumerate((firsts, lasts)):
        for j in range(quarter):
            for piece in group:
                post(OPEN + TURN * (j + quarter * part), 1, block_at(j), piece)
    over, events = {}, []
    while queue:
        queue.sort()
        at, step, sem, q = queue.pop(0)
        if step > 1:
            if (step - 1, sem, q) not in over:
                queue.append((queue[0][0] + 0.001, step, sem, q))
                continue
            at = max(at, over[step - 1, sem, q])
        over[step, sem, q] = at
        events.append((at, step, sem, q))
        if step < bits - 1 and q >= n >> (step + 2):
            post(at, step + 1, q, pieces[sem])
    begin = max(over[bits - 1, piece[3], 0] for piece in firsts)
    early_sems = [piece[3] for piece in firsts]
    done = [block_at(i) for i in range(quarter, n // 2 - 2)]
    events = sorted(e for e in events if not (e[1] == 1 and e[2] in early_sems and e[3] in done))

    def advance(at, step, sem, q):
        finish(pieces[sem], step, q)
        if step < bits - 1 and q >= n >> (step + 2):
            copy_of(pieces[sem], step + 1, q).start()

    while events and events[0][0] <= begin:
        advance(*events.pop(0))

    sums = jnp.concatenate(
        [early[0, HALF : HALF + CLASSES, :], early[0, HALF + CLASSES : TOP, :]], axis=1
    )
    count_row = early[0, TOP : TOP + 1, 0:CLASSES]
    eye = iota((CLASSES, CLASSES), 0) == iota((CLASSES, CLASSES), 1)
    counts = jnp.sum(jnp.where(eye, count_row, 0.0), axis=1, keepdims=True)
    total = jnp.sum(counts, axis=0, keepdims=True)
    centers = jnp.sum(sums, axis=0, keepdims=True) / total
    scaled = sums / jnp.maximum(counts, 1.0)
    row, col = iota((LANES, LANES), 0), iota((LANES, LANES), 1)
    ridge = jnp.where(row == col, RIDGE, 0.0)
    diag = early[0, TOP + 1 : TOP + 2, :]
    between = exact(scaled, sums, TN)
    shifts = (sums - counts * centers) / total
    square = unpack(early[0, 0:HALF, :], pltpu.roll(jnp.broadcast_to(diag, (GROUP, LANES)), HALF, 1)[0:1, :])
    rows = rows_of((square - between[:LANES, :LANES]) / total + ridge)
    for turned in range(LANES // WIDTH):
        while events and events[0][0] <= begin + STEP * turned:
            advance(*events.pop(0))
        rows = pivot(rows, WIDTH * turned, True)
    for event in events:
        advance(*event)

    inverse = jnp.concatenate(rows, axis=0)
    cross = (late[0, 0:LANES, :] - between[:LANES, LANES:]) / total
    square = unpack(late[0, LANES:LATE, :], diag)
    last = (square - between[LANES:, LANES:]) / total + ridge
    gain = exact(inverse, cross, NN)
    schur = last - exact(cross, gain, TN)
    right = shifts[:, LANES:] - exact(shifts[:, :LANES], gain, NN)
    left = exact(shifts[:, :LANES], inverse, NN)
    rows = rows_of(schur) + rows_of(right)
    for turned in range(LANES // WIDTH):
        rows = pivot(rows, WIDTH * turned, False)
    right = jnp.concatenate(rows[LANES // GROUP :], axis=0)
    left = left - exact(right, gain, NT)
    planes = jnp.concatenate([left, right], axis=1)
    planes_ref[...] = planes
    offsets = -jnp.sum(planes * centers, axis=1, keepdims=True)
    mine[...] = planes.astype(jnp.bfloat16)
    mine_offsets[:, 0:CLASSES] = jnp.sum(jnp.where(eye, offsets, 0.0), axis=0, keepdims=True)

    def far_copy(r):
        return pltpu.make_async_remote_copy(
            src_ref=mine,
            dst_ref=messages.at[r],
            send_sem=far_send.at[r],
            recv_sem=far_recv.at[r],
            device_id={"rows": device_at(me, r)},
        )

    def offset_copy(r):
        return pltpu.make_async_remote_copy(
            src_ref=mine_offsets,
            dst_ref=message_offsets.at[r],
            send_sem=near_send.at[r],
            recv_sem=near_recv.at[r],
            device_id={"rows": device_at(me, r)},
        )

    def score(r):
        q = sum(((r >> b) % 2) << (bits - 1 - b) for b in range(bits))
        node = nodes_ref[q]
        message, offset_row = (mine, mine_offsets) if r == 0 else (messages.at[r], message_offsets.at[r])
        offsets = jnp.sum(jnp.where(eye, offset_row[:, 0:CLASSES], 0.0), axis=1, keepdims=True)
        values = lax.dot_general(message[...], x_ref[node], NT, preferred_element_type=jnp.float32)
        values = values + offsets
        ids = ids_ref[pl.ds(node * tiles, tiles), :]
        for k in range(tiles):
            part = values[:, k * LANES : (k + 1) * LANES]
            scores[r, :, k * LANES : (k + 1) * LANES] = jnp.where(ids[k : k + 1, :] == node, part, 0.0)

    turns = list(range(1, n))
    for r in reversed(turns):
        far_copy(r).start()
        offset_copy(r).start()
    score(0)
    for r in turns:
        far_copy(r).wait_recv()
        offset_copy(r).wait_recv()
        score(r)
    for k in range(n):
        out_ref[:, k * seg : (k + 1) * seg] = scores[lax.bitwise_xor(owners_ref[k], me)]
    for step in range(bits):
        half = n >> (step + 1)
        for piece in pieces[2:] if step else wholes:
            for q in range(half, 2 * half):
                copy_of(piece, step, q).wait_send()
    for r in turns:
        far_copy(r).wait_send()
        offset_copy(r).wait_send()


def on_device(features, node_ids, labels, owners):
    row_count, feat = features.shape
    n = owners.shape[0]
    seg = row_count // n
    ids = node_ids.reshape(row_count // LANES, LANES)
    tags = labels.reshape(row_count // LANES, LANES)
    hbm = pl.BlockSpec(memory_space=pltpu.HBM)
    sems = len(EARLY_CUTS) + len(LATE_CUTS)
    whole = pl.BlockSpec(memory_space=pltpu.VMEM)
    dma = pltpu.SemaphoreType.DMA

    planes, scores = pl.pallas_call(
        functools.partial(tree_kernel, n),
        out_shape=(
            pltpu.VMEM((CLASSES, feat), jnp.float32),
            pltpu.VMEM((CLASSES, row_count), jnp.float32),
        ),
        in_specs=[hbm] * 4,
        out_specs=(whole, whole),
        scratch_shapes=[
            pltpu.SMEM((n,), jnp.int32),
            pltpu.SMEM((n,), jnp.int32),
            pltpu.VMEM((n, seg, feat), features.dtype),
            pltpu.VMEM(ids.shape, jnp.int32),
            pltpu.VMEM(ids.shape, jnp.int32),
            pltpu.VMEM((n, CLASSES, seg), jnp.bfloat16),
            pltpu.VMEM((n, GROUP, LANES), jnp.float32),
            pltpu.VMEM((n, EARLY, LANES), jnp.float32),
            pltpu.VMEM((n, EARLY, LANES), jnp.float32),
            pltpu.VMEM((n, LATE, LANES), jnp.float32),
            pltpu.VMEM((n, LATE, LANES), jnp.float32),
            pltpu.VMEM((CLASSES, feat), jnp.bfloat16),
            pltpu.VMEM((n, CLASSES, feat), jnp.bfloat16),
            pltpu.VMEM((1, LANES), jnp.float32),
            pltpu.VMEM((n, 1, LANES), jnp.float32),
            pltpu.VMEM((n, CLASSES, seg), jnp.float32),
            dma((4,)),
            dma((sems, n)),
            dma((sems, n)),
            dma((n,)),
            dma((n,)),
            dma((n,)),
            dma((n,)),
        ],
        compiler_params=pltpu.CompilerParams(
            collective_id=0, has_side_effects=True, vmem_limit_bytes=VMEM - 4 * CLASSES * (row_count + feat)
        ),
        name="tree",
    )(owners, features.reshape(n, seg, feat), ids, tags)

    return planes[None], scores


def solution(mesh):
    in_specs = (P(("leaf", "rows"), None), P(("leaf", "rows")), P(("leaf", "rows")), P("leaf"))
    out_specs = (P(("leaf", "rows"), None, None), P(None, ("leaf", "rows")))
    return jax.shard_map(
        on_device, mesh=mesh, in_specs=in_specs, out_specs=out_specs, check_vma=False
    )
```

```python
import functools
import jax
import jax.numpy as jnp
from jax import lax
from jax.experimental import pallas as pl
from jax.experimental.pallas import tpu as pltpu
from jax.sharding import PartitionSpec as P

CLASSES = 16
LANES = 128
HALF = LANES // 2
GROUP = 8
WIDTH = 4
BATCH = 4
RIDGE = 0.1
HIGHEST = lax.Precision.HIGHEST
NN = (((1,), (0,)), ((), ()))
TN = (((0,), (0,)), ((), ()))
NT = (((1,), (1,)), ((), ()))
TOP = HALF + 2 * CLASSES
EARLY = TOP + GROUP
LATE = LANES + HALF
EARLY_CUTS = (0, EARLY)
LATE_CUTS = (0, LANES, LATE)
RATE, NEAR, FAR, STEP = 0.009, 1.8, 2.6, 0.14
PAUSE, OPEN, TURN = 0.5, 4.0, 0.7
VMEM = 67043328


def iota(shape, dim):
    return lax.broadcasted_iota(jnp.int32, shape, dim)


def partner_of(me, bit):
    width = 1 << bit
    return me + width * (1 - 2 * ((me // width) % 2))


def device_at(me, r):
    bit = 0
    while r >> bit:
        if (r >> bit) % 2:
            me = partner_of(me, bit)
        bit += 1
    return me


def exact(a, b, dims):
    return lax.dot_general(a, b, dims, precision=HIGHEST, preferred_element_type=jnp.float32)


def pack(square):
    top, low = square[:HALF, :], square[HALF:, :]
    turned = pltpu.roll(low, HALF, 1)
    row, col = iota((HALF, LANES), 0), iota((HALF, LANES), 1)
    packed = jnp.where((row >= col) | (col >= HALF), top, turned)
    diag = jnp.sum(jnp.where(row + HALF == col, low, 0.0), axis=0, keepdims=True)
    return packed, diag


def unpack(packed, diag):
    row, col = iota((HALF, LANES), 0), iota((HALF, LANES), 1)
    turned = jnp.concatenate([packed, jnp.zeros_like(packed)], axis=0).T
    top = jnp.where((row >= col) | (col >= HALF), packed, turned[:HALF, :])
    last = jnp.where(row < col, packed, jnp.where(row == col, diag, turned[:HALF, :]))
    low = jnp.where(col < HALF, turned[HALF:, :], pltpu.roll(last, HALF, 1))
    return jnp.concatenate([top, low], axis=0)


def mark(node, ids_ref, labels_ref, hot_ref, tally_ref):
    seg = hot_ref.shape[2]
    tiles = seg // LANES
    tags = labels_ref[pl.ds(node * tiles, tiles), :]
    live = ids_ref[pl.ds(node * tiles, tiles), :] == node
    length = jnp.sum(live.astype(jnp.float32), axis=(0, 1), keepdims=True)
    tags = jnp.where(live, tags, -1)
    hot = jnp.concatenate(
        [tags[k : k + 1, :] == iota((CLASSES, LANES), 0) for k in range(tiles)], axis=1
    )
    hot = hot.astype(jnp.float32).astype(jnp.bfloat16)
    counts = lax.dot_general(
        jnp.ones((GROUP, seg), jnp.bfloat16), hot, NT, preferred_element_type=jnp.float32
    )
    counts = jnp.concatenate([counts, jnp.zeros((GROUP, LANES - CLASSES), jnp.float32)], axis=1)
    hot_ref[node] = hot
    tally_ref[node] = jnp.where(iota((GROUP, LANES), 0) == 0, counts, length)


def one_partial(node, q, x_ref, hot_ref, tally_ref, early, late):
    seg, feat = x_ref.shape[1:]
    tally = tally_ref[node]
    x = x_ref[node]
    position = iota((seg, feat), 0).astype(jnp.float32)
    length = jnp.concatenate([tally[1:2, :]] * (feat // LANES), axis=1)
    x = jnp.where(position < length, x, jnp.zeros((), x.dtype))
    moment = lax.dot_general(x, x, TN, preferred_element_type=jnp.float32)
    sums = jnp.dot(hot_ref[node], x, preferred_element_type=jnp.float32)
    packed, diag = pack(moment[:LANES, :LANES])
    early[q, 0:HALF, :] = packed
    early[q, HALF : HALF + CLASSES, :] = sums[:, :LANES]
    early[q, HALF + CLASSES : TOP, :] = sums[:, LANES:]
    packed, other = pack(moment[LANES:, LANES:])
    diag = diag + pltpu.roll(jnp.broadcast_to(other, (GROUP, LANES)), HALF, 1)
    early[q, TOP:EARLY, :] = jnp.where(iota((GROUP, LANES), 0) == 0, tally, diag)
    top, low = moment[:HALF, LANES:], moment[HALF:LANES, LANES:]
    left = iota((HALF, LANES), 1) < HALF
    late[q, 0:HALF, :] = jnp.where(left, top, pltpu.roll(low, HALF, 1))
    late[q, HALF:LANES, :] = packed
    late[q, LANES:LATE, :] = jnp.where(left, pltpu.roll(top, HALF, 1), low)


def lane_of(x, lane):
    return jnp.broadcast_to(x[:, lane : lane + 1], x.shape)


def pivot(rows, at, whole):
    group, base = at // GROUP, at % GROUP
    lanes = iota((1, LANES), 1)
    pivots = rows[group]
    spread = [lane_of(pivots, at + u) for u in range(4)]
    d = [[spread[u][base + t : base + t + 1, :] for u in range(4)] for t in range(4)]
    a, b, c = d[0][0], d[0][1], d[1][1]
    inv = 1.0 / (a * c - b * b)
    p00, p01, p11 = c * inv, -b * inv, a * inv
    q00, q01, q10, q11 = d[0][2], d[0][3], d[1][2], d[1][3]
    t00, t01 = p00 * q00 + p01 * q10, p00 * q01 + p01 * q11
    t10, t11 = p01 * q00 + p11 * q10, p01 * q01 + p11 * q11
    s00 = d[2][2] - (q00 * t00 + q10 * t10)
    s01 = d[2][3] - (q00 * t01 + q10 * t11)
    s11 = d[3][3] - (q01 * t01 + q11 * t11)
    inv = 1.0 / (s00 * s11 - s01 * s01)
    h00, h01, h11 = s11 * inv, -s01 * inv, s00 * inv
    u00, u01 = t00 * h00 + t01 * h01, t00 * h01 + t01 * h11
    u10, u11 = t10 * h00 + t11 * h01, t10 * h01 + t11 * h11
    e00 = p00 + u00 * t00 + u01 * t01
    e01 = p01 + u00 * t10 + u01 * t11
    e11 = p11 + u10 * t10 + u11 * t11
    dinv = [
        [e00, e01, -u00, -u01],
        [e01, e11, -u10, -u11],
        [-u00, -u10, h00, h01],
        [-u01, -u11, h01, h11],
    ]
    inside = (lanes >= at) & (lanes < at + 4)
    near = [
        jnp.where(inside, jnp.where(lanes == at + t, -1.0, 0.0), pivots[base + t : base + t + 1, :])
        for t in range(4)
    ]
    mix = lambda t: (dinv[t][0] * near[0] + dinv[t][1] * near[1]) + (
        dinv[t][2] * near[2] + dinv[t][3] * near[3]
    )
    w = [jnp.broadcast_to(mix(t), (GROUP, LANES)) for t in range(4)]
    inside = jnp.broadcast_to(inside, (GROUP, LANES))
    depth = iota((GROUP, LANES), 0)
    out = list(rows)
    first = 0 if whole else (group if base == 0 else group + 1)
    for g in range(first, len(rows)):
        x = rows[g]
        k = [lane_of(x, at + u) for u in range(4)]
        gone = inside
        if whole and g == group:
            own = (depth >= base) & (depth < base + 4)
            k = [jnp.where(own, jnp.where(depth == base + u, 1.0, 0.0), k[u]) for u in range(4)]
            gone = inside | own
        x = jnp.where(gone, 0.0, x)
        out[g] = x - ((k[0] * w[0] + k[1] * w[1]) + (k[2] * w[2] + k[3] * w[3]))
    return out


def rows_of(x):
    return [x[g : g + GROUP, :] for g in range(0, x.shape[0], GROUP)]


def tree_kernel(
    n,
    owners_hbm,
    x_hbm,
    ids_hbm,
    labels_hbm,
    planes_ref,
    out_ref,
    owners_ref,
    nodes_ref,
    x_ref,
    ids_ref,
    labels_ref,
    hot_ref,
    tally_ref,
    early,
    early_in,
    late,
    late_in,
    mine,
    messages,
    mine_offsets,
    message_offsets,
    scores,
    load_sems,
    sum_send,
    sum_recv,
    far_send,
    far_recv,
    near_send,
    near_recv,
):
    bits = n.bit_length() - 1
    seg, feat = x_ref.shape[1:]
    tiles = seg // LANES
    me = lax.axis_index("rows")
    barrier = pltpu.get_barrier_semaphore()
    pairs = [(owners_hbm, owners_ref), (ids_hbm, ids_ref), (labels_hbm, labels_ref), (x_hbm, x_ref)]
    loads = [pltpu.make_async_copy(a, b, load_sems.at[k]) for k, (a, b) in enumerate(pairs)]
    for load in loads:
        load.start()
    for bit in range(bits):
        pl.semaphore_signal(barrier, inc=1, device_id={"rows": partner_of(me, bit)})
    for load in loads[:-1]:
        load.wait()

    def prepare(k, carry):
        mark(k, ids_ref, labels_ref, hot_ref, tally_ref)
        return carry

    lax.fori_loop(0, n, prepare, 0, unroll=8)
    loads[-1].wait()
    pl.semaphore_wait(barrier, bits)

    wholes = [(0, 0, EARLY, 0), (1, 0, LATE, 1)]
    pieces = list(wholes)
    for part, cuts in enumerate((EARLY_CUTS, LATE_CUTS)):
        pieces += [(part, lo, hi - lo, len(pieces) + k) for k, (lo, hi) in enumerate(zip(cuts, cuts[1:]))]
    firsts = [p for p in pieces[2:] if p[0] == 0]
    middles = [p for p in pieces[2:] if p[0] == 1 and p[1] < LANES]
    lasts = [p for p in pieces[2:] if p[0] == 1 and p[1] >= LANES]
    held, landed = (early, late), (early_in, late_in)

    def copy_of(piece, step, q):
        part, low, size, sem = piece
        return pltpu.make_async_remote_copy(
            src_ref=held[part].at[q, pl.ds(low, size)],
            dst_ref=landed[part].at[q, pl.ds(low, size)],
            send_sem=sum_send.at[sem, q],
            recv_sem=sum_recv.at[sem, q],
            device_id={"rows": partner_of(me, step)},
        )

    def partial(q):
        slot = 0
        for b in range(bits):
            mine, theirs = (me // (1 << b)) % 2, (q // (1 << (bits - 1 - b))) % 2
            slot = slot + (1 << b) * ((mine + theirs) % 2)
        node = 0
        for k in range(n):
            node = jnp.where(owners_ref[k] == slot, k, node)
        nodes_ref[q] = node
        one_partial(node, q, x_ref, hot_ref, tally_ref, early, late)

    def finish(piece, step, q):
        half = n >> (step + 1)
        copy_of(piece, step, q + half).wait_recv()
        part, low, size, sem = piece
        rows = pl.ds(low, size)
        held[part][q, rows] = held[part][q, rows] + landed[part][q + half, rows]

    quarter = n // 4

    def turn(i):
        low = quarter - 1 - i % quarter
        for b in range(bits - 2):
            yield (low // (1 << b)) % 2, bits - 3 - b
        yield 1 - i // quarter, bits - 2

    def block_at(i):
        return sum(bit * (1 << place) for bit, place in turn(i))

    def pair(i, carry):
        q = block_at(i)
        partial(q + n // 2)
        partial(q)
        for piece in wholes:
            copy_of(piece, 0, q + n // 2).start()

        @pl.when(i >= 1)
        def _():
            before = block_at(i - 1)
            finish(wholes[0], 0, before)

            @pl.when(i - 1 < quarter)
            def _():
                for piece in firsts:
                    copy_of(piece, 1, before).start()

            finish(wholes[1], 0, before)

        @pl.when(i >= quarter + 1)
        def _():
            for piece in middles:
                copy_of(piece, 1, block_at(i - 1 - quarter)).start()

        @pl.when(i >= quarter + 2)
        def _():
            before = block_at(i - 2)
            for piece in firsts:
                finish(piece, 1, before)

            @pl.when(before >= n // 8)
            def _():
                for piece in firsts:
                    copy_of(piece, 2, before).start()

        return carry

    lax.fori_loop(0, n // 2, pair, 0)
    finish(wholes[0], 0, 0)
    for piece in middles:
        copy_of(piece, 1, block_at(quarter - 1)).start()
    for j in range(quarter):
        for piece in lasts:
            copy_of(piece, 1, block_at(j)).start()
    finish(wholes[1], 0, 0)

    free = [0.0] * bits
    queue = []

    def post(at, step, q, piece):
        begin = max(at, free[step])
        free[step] = begin + RATE * piece[2]
        queue.append((free[step] + (NEAR if step < bits - 1 else FAR), step, piece[3], q - (n >> (step + 1))))

    for part, group in enumerate((firsts, middles, lasts)):
        for j in range(quarter):
            for piece in group:
                post(OPEN + TURN * (j + quarter * part), 1, block_at(j), piece)
    over, events = {}, []
    while queue:
        queue.sort()
        at, step, sem, q = queue.pop(0)
        if step > 1:
            if (step - 1, sem, q) not in over:
                queue.append((queue[0][0] + 0.001, step, sem, q))
                continue
            at = max(at, over[step - 1, sem, q])
        over[step, sem, q] = at
        events.append((at, step, sem, q))
        if step < bits - 1 and q >= n >> (step + 2):
            post(at, step + 1, q, pieces[sem])
    begin = max(over[bits - 1, piece[3], 0] for piece in firsts)
    arrive = max(over[bits - 1, piece[3], 0] for piece in middles)
    resume = max(arrive, begin + STEP * (LANES // WIDTH)) + PAUSE
    early_sems = [piece[3] for piece in firsts]
    done = [block_at(i) for i in range(quarter, n // 2 - 2)]
    events = sorted(e for e in events if not (e[1] == 1 and e[2] in early_sems and e[3] in done))

    def advance(at, step, sem, q):
        finish(pieces[sem], step, q)
        if step < bits - 1 and q >= n >> (step + 2):
            copy_of(pieces[sem], step + 1, q).start()

    while events and events[0][0] <= begin:
        advance(*events.pop(0))

    sums = jnp.concatenate(
        [early[0, HALF : HALF + CLASSES, :], early[0, HALF + CLASSES : TOP, :]], axis=1
    )
    count_row = early[0, TOP : TOP + 1, 0:CLASSES]
    eye = iota((CLASSES, CLASSES), 0) == iota((CLASSES, CLASSES), 1)
    counts = jnp.sum(jnp.where(eye, count_row, 0.0), axis=1, keepdims=True)
    total = jnp.sum(counts, axis=0, keepdims=True)
    centers = jnp.sum(sums, axis=0, keepdims=True) / total
    scaled = sums / jnp.maximum(counts, 1.0)
    row, col = iota((LANES, LANES), 0), iota((LANES, LANES), 1)
    ridge = jnp.where(row == col, RIDGE, 0.0)
    diag = early[0, TOP + 1 : TOP + 2, :]
    between = exact(scaled, sums, TN)
    shifts = (sums - counts * centers) / total
    square = unpack(early[0, 0:HALF, :], pltpu.roll(jnp.broadcast_to(diag, (GROUP, LANES)), HALF, 1)[0:1, :])
    rows = rows_of((square - between[:LANES, :LANES]) / total + ridge)
    for turned in range(LANES // WIDTH):
        while events and events[0][0] <= begin + STEP * turned:
            advance(*events.pop(0))
        rows = pivot(rows, WIDTH * turned, True)
    while events and events[0][0] <= arrive:
        advance(*events.pop(0))

    col = iota((LANES, LANES), 1)
    kept = col < HALF
    turn_over = lambda x: pltpu.roll(x, HALF, 1)
    stack = lambda x: jnp.concatenate([x, turn_over(x)], axis=0)
    inverse = jnp.concatenate(rows, axis=0)
    beside, below = between[:LANES, LANES:], between[LANES:, LANES:]
    last = (unpack(late[0, HALF:LANES, :], diag) - below) / total + ridge
    cross = jnp.where(kept, (stack(late[0, 0:HALF, :]) - beside) / total, 0.0)
    gain = exact(inverse, cross, NN)
    rows = rows_of(last[:HALF, :] - exact(cross[:, :HALF], gain, TN))
    far = shifts[:, LANES:] - exact(shifts[:, :LANES], gain, NN)
    left = exact(shifts[:, :LANES], inverse, NN)
    for turned in range(HALF // WIDTH):
        while events and events[0][0] <= resume + STEP * turned:
            advance(*events.pop(0))
        rows = pivot(rows, WIDTH * turned, True)
    for event in events:
        advance(*event)

    middle = jnp.concatenate(rows, axis=0)[:, :HALF]
    far = far[:, :HALF]
    near = exact(far, middle, NN)
    other = (stack(late[0, LANES:LATE, :]) - turn_over(beside)) / total
    other = jnp.where(kept, other, 0.0)
    pull = exact(inverse, other, NN)
    both = jnp.where(kept, cross, turn_over(other))
    rest = turn_over(last) - exact(both, pull, TN)
    side = rest[:HALF, :]
    link = exact(middle, side, NN)
    rows = rows_of(rest[HALF:, :] - exact(side[:, :HALF], link, TN))
    end = turn_over(shifts[:, LANES:]) - exact(shifts[:, :LANES], pull, NN) - exact(far, link, NN)
    rows = rows + rows_of(end)
    gains = jnp.where(kept, gain, turn_over(pull))
    for turned in range(HALF // WIDTH):
        rows = pivot(rows, WIDTH * turned, False)
    end = jnp.concatenate(rows[HALF // GROUP :], axis=0)[:, :HALF]
    right = jnp.concatenate([near - exact(end, link[:, :HALF], NT), end], axis=1)
    left = left - exact(right, gains, NT)
    planes = jnp.concatenate([left, right], axis=1)
    planes_ref[...] = planes
    offsets = -jnp.sum(planes * centers, axis=1, keepdims=True)
    mine[...] = planes.astype(jnp.bfloat16)
    mine_offsets[:, 0:CLASSES] = jnp.sum(jnp.where(eye, offsets, 0.0), axis=0, keepdims=True)

    def far_copy(r):
        return pltpu.make_async_remote_copy(
            src_ref=mine,
            dst_ref=messages.at[r],
            send_sem=far_send.at[r],
            recv_sem=far_recv.at[r],
            device_id={"rows": device_at(me, r)},
        )

    def offset_copy(r):
        return pltpu.make_async_remote_copy(
            src_ref=mine_offsets,
            dst_ref=message_offsets.at[r],
            send_sem=near_send.at[r],
            recv_sem=near_recv.at[r],
            device_id={"rows": device_at(me, r)},
        )

    def score(r):
        q = sum(((r >> b) % 2) << (bits - 1 - b) for b in range(bits))
        node = nodes_ref[q]
        message, offset_row = (mine, mine_offsets) if r == 0 else (messages.at[r], message_offsets.at[r])
        offsets = jnp.sum(jnp.where(eye, offset_row[:, 0:CLASSES], 0.0), axis=1, keepdims=True)
        values = lax.dot_general(message[...], x_ref[node], NT, preferred_element_type=jnp.float32)
        values = values + offsets
        ids = ids_ref[pl.ds(node * tiles, tiles), :]
        for k in range(tiles):
            part = values[:, k * LANES : (k + 1) * LANES]
            scores[r, :, k * LANES : (k + 1) * LANES] = jnp.where(ids[k : k + 1, :] == node, part, 0.0)

    turns = list(range(1, n))
    for r in reversed(turns):
        far_copy(r).start()
        offset_copy(r).start()
    score(0)
    for start in range(0, n, BATCH):
        batch = range(max(start, 1), start + BATCH)
        for r in batch:
            far_copy(r).wait_recv()
            offset_copy(r).wait_recv()
        for r in batch:
            score(r)
    for k in range(n):
        out_ref[:, k * seg : (k + 1) * seg] = scores[lax.bitwise_xor(owners_ref[k], me)]
    for step in range(bits):
        half = n >> (step + 1)
        for piece in pieces[2:] if step else wholes:
            for q in range(half, 2 * half):
                copy_of(piece, step, q).wait_send()
    for r in turns:
        far_copy(r).wait_send()
        offset_copy(r).wait_send()


def on_device(features, node_ids, labels, owners):
    row_count, feat = features.shape
    n = owners.shape[0]
    seg = row_count // n
    ids = node_ids.reshape(row_count // LANES, LANES)
    tags = labels.reshape(row_count // LANES, LANES)
    hbm = pl.BlockSpec(memory_space=pltpu.HBM)
    sems = len(EARLY_CUTS) + len(LATE_CUTS)
    whole = pl.BlockSpec(memory_space=pltpu.VMEM)
    dma = pltpu.SemaphoreType.DMA

    planes, scores = pl.pallas_call(
        functools.partial(tree_kernel, n),
        out_shape=(
            pltpu.VMEM((CLASSES, feat), jnp.float32),
            pltpu.VMEM((CLASSES, row_count), jnp.float32),
        ),
        in_specs=[hbm] * 4,
        out_specs=(whole, whole),
        scratch_shapes=[
            pltpu.SMEM((n,), jnp.int32),
            pltpu.SMEM((n,), jnp.int32),
            pltpu.VMEM((n, seg, feat), features.dtype),
            pltpu.VMEM(ids.shape, jnp.int32),
            pltpu.VMEM(ids.shape, jnp.int32),
            pltpu.VMEM((n, CLASSES, seg), jnp.bfloat16),
            pltpu.VMEM((n, GROUP, LANES), jnp.float32),
            pltpu.VMEM((n, EARLY, LANES), jnp.float32),
            pltpu.VMEM((n, EARLY, LANES), jnp.float32),
            pltpu.VMEM((n, LATE, LANES), jnp.float32),
            pltpu.VMEM((n, LATE, LANES), jnp.float32),
            pltpu.VMEM((CLASSES, feat), jnp.bfloat16),
            pltpu.VMEM((n, CLASSES, feat), jnp.bfloat16),
            pltpu.VMEM((1, LANES), jnp.float32),
            pltpu.VMEM((n, 1, LANES), jnp.float32),
            pltpu.VMEM((n, CLASSES, seg), jnp.float32),
            dma((4,)),
            dma((sems, n)),
            dma((sems, n)),
            dma((n,)),
            dma((n,)),
            dma((n,)),
            dma((n,)),
        ],
        compiler_params=pltpu.CompilerParams(
            collective_id=0, has_side_effects=True, vmem_limit_bytes=VMEM - 4 * CLASSES * (row_count + feat)
        ),
        name="tree",
    )(owners, features.reshape(n, seg, feat), ids, tags)

    return planes[None], scores


def solution(mesh):
    in_specs = (P(("leaf", "rows"), None), P(("leaf", "rows")), P(("leaf", "rows")), P("leaf"))
    out_specs = (P(("leaf", "rows"), None, None), P(None, ("leaf", "rows")))
    return jax.shard_map(
        on_device, mesh=mesh, in_specs=in_specs, out_specs=out_specs, check_vma=False
    )
```

```python
import functools
import jax
import jax.numpy as jnp
from jax import lax
from jax.experimental import pallas as pl
from jax.experimental.pallas import tpu as pltpu
from jax.sharding import PartitionSpec as P

CLASSES = 16
LANES = 128
HALF = LANES // 2
GROUP = 8
WIDTH = 8
BATCH = 4
CHUNKS = 8
RIDGE = 0.1
HIGHEST = lax.Precision.HIGHEST
NN = (((1,), (0,)), ((), ()))
TN = (((0,), (0,)), ((), ()))
NT = (((1,), (1,)), ((), ()))
TOP = HALF + 2 * CLASSES
EARLY = TOP + GROUP
LATE = LANES + HALF
EARLY_CUTS = (0, EARLY)
LATE_CUTS = (0, LANES, LATE)
RATE, NEAR, FAR, STEP = 0.0085, 1.8, 2.6, 0.28
PAUSE, OPEN, TURN = 0.5, 4.0, 0.7
VMEM = 67043328


def iota(shape, dim):
    return lax.broadcasted_iota(jnp.int32, shape, dim)


def partner_of(me, bit):
    width = 1 << bit
    return me + width * (1 - 2 * ((me // width) % 2))


def device_at(me, r):
    bit = 0
    while r >> bit:
        if (r >> bit) % 2:
            me = partner_of(me, bit)
        bit += 1
    return me


def exact(a, b, dims):
    return lax.dot_general(a, b, dims, precision=HIGHEST, preferred_element_type=jnp.float32)


def pack(square):
    top, low = square[:HALF, :], square[HALF:, :]
    turned = pltpu.roll(low, HALF, 1)
    row, col = iota((HALF, LANES), 0), iota((HALF, LANES), 1)
    packed = jnp.where((row >= col) | (col >= HALF), top, turned)
    diag = jnp.sum(jnp.where(row + HALF == col, low, 0.0), axis=0, keepdims=True)
    return packed, diag


def unpack(packed, diag):
    row, col = iota((HALF, LANES), 0), iota((HALF, LANES), 1)
    turned = jnp.concatenate([packed, jnp.zeros_like(packed)], axis=0).T
    top = jnp.where((row >= col) | (col >= HALF), packed, turned[:HALF, :])
    last = jnp.where(row < col, packed, jnp.where(row == col, diag, turned[:HALF, :]))
    low = jnp.where(col < HALF, turned[HALF:, :], pltpu.roll(last, HALF, 1))
    return jnp.concatenate([top, low], axis=0)


def mark(node, ids_ref, labels_ref, hot_ref, tally_ref):
    seg = hot_ref.shape[2]
    tiles = seg // LANES
    tags = labels_ref[pl.ds(node * tiles, tiles), :]
    live = ids_ref[pl.ds(node * tiles, tiles), :] == node
    length = jnp.sum(live.astype(jnp.float32), axis=(0, 1), keepdims=True)
    tags = jnp.where(live, tags, -1)
    hot = jnp.concatenate(
        [tags[k : k + 1, :] == iota((CLASSES, LANES), 0) for k in range(tiles)], axis=1
    )
    hot = hot.astype(jnp.float32).astype(jnp.bfloat16)
    counts = lax.dot_general(
        jnp.ones((GROUP, seg), jnp.bfloat16), hot, NT, preferred_element_type=jnp.float32
    )
    counts = jnp.concatenate([counts, jnp.zeros((GROUP, LANES - CLASSES), jnp.float32)], axis=1)
    hot_ref[node] = hot
    tally_ref[node] = jnp.where(iota((GROUP, LANES), 0) == 0, counts, length)


def one_partial(node, q, x_ref, hot_ref, tally_ref, early, late):
    seg, feat = x_ref.shape[1:]
    tally = tally_ref[node]
    x = x_ref[node]
    position = iota((seg, feat), 0).astype(jnp.float32)
    length = jnp.concatenate([tally[1:2, :]] * (feat // LANES), axis=1)
    x = jnp.where(position < length, x, jnp.zeros((), x.dtype))
    moment = lax.dot_general(x, x, TN, preferred_element_type=jnp.float32)
    sums = jnp.dot(hot_ref[node], x, preferred_element_type=jnp.float32)
    packed, diag = pack(moment[:LANES, :LANES])
    early[q, 0:HALF, :] = packed
    early[q, HALF : HALF + CLASSES, :] = sums[:, :LANES]
    early[q, HALF + CLASSES : TOP, :] = sums[:, LANES:]
    packed, other = pack(moment[LANES:, LANES:])
    diag = diag + pltpu.roll(jnp.broadcast_to(other, (GROUP, LANES)), HALF, 1)
    early[q, TOP:EARLY, :] = jnp.where(iota((GROUP, LANES), 0) == 0, tally, diag)
    top, low = moment[:HALF, LANES:], moment[HALF:LANES, LANES:]
    left = iota((HALF, LANES), 1) < HALF
    late[q, 0:HALF, :] = jnp.where(left, top, pltpu.roll(low, HALF, 1))
    late[q, HALF:LANES, :] = packed
    late[q, LANES:LATE, :] = jnp.where(left, pltpu.roll(top, HALF, 1), low)


def lane_of(x, lane):
    return jnp.broadcast_to(x[:, lane : lane + 1], x.shape)


def dot(a, b):
    terms = [x * y for x, y in zip(a, b)]
    while len(terms) > 1:
        terms = [terms[k] + terms[k + 1] for k in range(0, len(terms), 2)]
    return terms[0]


def invert2(a, b, c):
    inv = 1.0 / (a * c - b * b)
    return c * inv, -b * inv, a * inv


def parts4(d):
    p00, p01, p11 = invert2(d[0][0], d[0][1], d[1][1])
    q = [[d[0][2], d[0][3]], [d[1][2], d[1][3]]]
    t = [
        [p00 * q[0][j] + p01 * q[1][j] for j in (0, 1)],
        [p01 * q[0][j] + p11 * q[1][j] for j in (0, 1)],
    ]
    s = lambda i, j: d[2 + i][2 + j] - (q[0][i] * t[0][j] + q[1][i] * t[1][j])
    h00, h01, h11 = invert2(s(0, 0), s(0, 1), s(1, 1))
    return p00, p01, p11, t, h00, h01, h11


def inverse4(d):
    p00, p01, p11, t, h00, h01, h11 = parts4(d)
    u = [[t[i][0] * h00 + t[i][1] * h01, t[i][0] * h01 + t[i][1] * h11] for i in (0, 1)]
    e = lambda p, i, j: p + (u[i][0] * t[j][0] + u[i][1] * t[j][1])
    e00, e01, e11 = e(p00, 0, 0), e(p01, 0, 1), e(p11, 1, 1)
    return [
        [e00, e01, -u[0][0], -u[0][1]],
        [e01, e11, -u[1][0], -u[1][1]],
        [-u[0][0], -u[1][0], h00, h01],
        [-u[0][1], -u[1][1], h01, h11],
    ]


def solve4(d, n):
    p00, p01, p11, t, h00, h01, h11 = parts4(d)
    m2 = n[2] - (t[0][0] * n[0] + t[1][0] * n[1])
    m3 = n[3] - (t[0][1] * n[0] + t[1][1] * n[1])
    w2, w3 = h00 * m2 + h01 * m3, h01 * m2 + h11 * m3
    w0 = (p00 * n[0] + p01 * n[1]) - (t[0][0] * w2 + t[0][1] * w3)
    w1 = (p01 * n[0] + p11 * n[1]) - (t[1][0] * w2 + t[1][1] * w3)
    return [w0, w1, w2, w3]


def solve8(d, n):
    four = range(4)
    p = inverse4([row[:4] for row in d[:4]])
    q = [row[4:] for row in d[:4]]
    t = [[dot(p[i], [q[k][j] for k in four]) for j in four] for i in four]
    s = [[None] * 4 for i in four]
    for i in four:
        for j in range(i, 4):
            s[i][j] = d[4 + i][4 + j] - dot([q[k][i] for k in four], [t[k][j] for k in four])
    m = [n[4 + i] - dot([t[k][i] for k in four], n[:4]) for i in four]
    low = solve4(s, m)
    return [dot(p[i], n[:4]) - dot(t[i], low) for i in four] + low


def pivot(rows, at, whole):
    group = at // GROUP
    shape = (GROUP, LANES)
    lanes, lane, depth = iota(shape, 1), iota((1, LANES), 1), iota(shape, 0)
    span = range(WIDTH)
    pivots = rows[group]
    spread = [lane_of(pivots, at + u) for u in span]
    d = [[spread[u][t : t + 1, :] if u >= t else None for u in span] for t in span]
    inside, within = (lanes >= at) & (lanes < at + WIDTH), (lane >= at) & (lane < at + WIDTH)
    near = [
        jnp.where(within, jnp.where(lane == at + t, -1.0, 0.0), pivots[t : t + 1, :]) for t in span
    ]
    w = [jnp.broadcast_to(x, shape) for x in solve8(d, near)]
    out = list(rows)
    if whole:
        own = w[0]
        for t in span:
            own = jnp.where(depth == t, w[t], own)
        out[group] = -own
    for g in range(0 if whole else group + 1, len(rows)):
        if g != group:
            k = [lane_of(rows[g], at + u) for u in span]
            out[g] = jnp.where(inside, 0.0, rows[g]) - dot(k, w)
    return out


def rows_of(x):
    return [x[g : g + GROUP, :] for g in range(0, x.shape[0], GROUP)]


def tree_kernel(
    n,
    owners_hbm,
    x_hbm,
    ids_hbm,
    labels_hbm,
    planes_ref,
    out_ref,
    owners_ref,
    nodes_ref,
    x_ref,
    ids_ref,
    labels_ref,
    hot_ref,
    tally_ref,
    early,
    early_in,
    late,
    late_in,
    mine,
    messages,
    mine_offsets,
    message_offsets,
    scores,
    load_sems,
    sum_send,
    sum_recv,
    far_send,
    far_recv,
    near_send,
    near_recv,
):
    bits = n.bit_length() - 1
    seg, feat = x_ref.shape[1:]
    tiles = seg // LANES
    me = lax.axis_index("rows")
    barrier = pltpu.get_barrier_semaphore()
    pairs = [(owners_hbm, owners_ref), (ids_hbm, ids_ref), (labels_hbm, labels_ref)]
    part = n // CHUNKS
    for k in range(CHUNKS):
        pairs.append((x_hbm.at[pl.ds(k * part, part)], x_ref.at[pl.ds(k * part, part)]))
    loads = [pltpu.make_async_copy(a, b, load_sems.at[k]) for k, (a, b) in enumerate(pairs)]
    for load in loads:
        load.start()
    for bit in range(bits):
        pl.semaphore_signal(barrier, inc=1, device_id={"rows": partner_of(me, bit)})
    for load in loads[:3]:
        load.wait()

    def prepare(k, carry):
        mark(k, ids_ref, labels_ref, hot_ref, tally_ref)
        return carry

    lax.fori_loop(0, n, prepare, 0, unroll=8)
    for load in loads[3:]:
        load.wait()
    pl.semaphore_wait(barrier, bits)

    wholes = [(0, 0, EARLY, 0), (1, 0, LATE, 1)]
    pieces = list(wholes)
    for part, cuts in enumerate((EARLY_CUTS, LATE_CUTS)):
        pieces += [(part, lo, hi - lo, len(pieces) + k) for k, (lo, hi) in enumerate(zip(cuts, cuts[1:]))]
    firsts = [p for p in pieces[2:] if p[0] == 0]
    middles = [p for p in pieces[2:] if p[0] == 1 and p[1] < LANES]
    lasts = [p for p in pieces[2:] if p[0] == 1 and p[1] >= LANES]
    held, landed = (early, late), (early_in, late_in)

    def copy_of(piece, step, q):
        part, low, size, sem = piece
        return pltpu.make_async_remote_copy(
            src_ref=held[part].at[q, pl.ds(low, size)],
            dst_ref=landed[part].at[q, pl.ds(low, size)],
            send_sem=sum_send.at[sem, q],
            recv_sem=sum_recv.at[sem, q],
            device_id={"rows": partner_of(me, step)},
        )

    def partial(q):
        slot = 0
        for b in range(bits):
            mine, theirs = (me // (1 << b)) % 2, (q // (1 << (bits - 1 - b))) % 2
            slot = slot + (1 << b) * ((mine + theirs) % 2)
        node = 0
        for k in range(n):
            node = jnp.where(owners_ref[k] == slot, k, node)
        nodes_ref[q] = node
        one_partial(node, q, x_ref, hot_ref, tally_ref, early, late)

    def finish(piece, step, q):
        half = n >> (step + 1)
        copy_of(piece, step, q + half).wait_recv()
        part, low, size, sem = piece
        rows = pl.ds(low, size)
        held[part][q, rows] = held[part][q, rows] + landed[part][q + half, rows]

    quarter = n // 4

    def turn(i):
        low = quarter - 1 - i % quarter
        for b in range(bits - 2):
            yield (low // (1 << b)) % 2, bits - 3 - b
        yield 1 - i // quarter, bits - 2

    def block_at(i):
        return sum(bit * (1 << place) for bit, place in turn(i))

    def pair(i, carry):
        q = block_at(i)
        partial(q + n // 2)
        partial(q)
        for piece in wholes:
            copy_of(piece, 0, q + n // 2).start()

        @pl.when(i >= 1)
        def _():
            before = block_at(i - 1)
            finish(wholes[0], 0, before)

            @pl.when(i - 1 < quarter)
            def _():
                for piece in firsts:
                    copy_of(piece, 1, before).start()

            finish(wholes[1], 0, before)

        @pl.when(i >= quarter + 1)
        def _():
            for piece in middles:
                copy_of(piece, 1, block_at(i - 1 - quarter)).start()

        @pl.when(i >= quarter + 2)
        def _():
            before = block_at(i - 2)
            for piece in firsts:
                finish(piece, 1, before)

            @pl.when(before >= n // 8)
            def _():
                for piece in firsts:
                    copy_of(piece, 2, before).start()

        return carry

    lax.fori_loop(0, n // 2, pair, 0)
    finish(wholes[0], 0, 0)
    for piece in middles:
        copy_of(piece, 1, block_at(quarter - 1)).start()
    for j in range(quarter):
        for piece in lasts:
            copy_of(piece, 1, block_at(j)).start()
    finish(wholes[1], 0, 0)

    free = [0.0] * bits
    queue = []

    def post(at, step, q, piece):
        begin = max(at, free[step])
        free[step] = begin + RATE * piece[2]
        queue.append((free[step] + (NEAR if step < bits - 1 else FAR), step, piece[3], q - (n >> (step + 1))))

    for part, group in enumerate((firsts, middles, lasts)):
        for j in range(quarter):
            for piece in group:
                post(OPEN + TURN * (j + quarter * part), 1, block_at(j), piece)
    over, events = {}, []
    while queue:
        queue.sort()
        at, step, sem, q = queue.pop(0)
        if step > 1:
            if (step - 1, sem, q) not in over:
                queue.append((queue[0][0] + 0.001, step, sem, q))
                continue
            at = max(at, over[step - 1, sem, q])
        over[step, sem, q] = at
        events.append((at, step, sem, q))
        if step < bits - 1 and q >= n >> (step + 2):
            post(at, step + 1, q, pieces[sem])
    begin = max(over[bits - 1, piece[3], 0] for piece in firsts)
    arrive = max(over[bits - 1, piece[3], 0] for piece in middles)
    resume = max(arrive, begin + STEP * (LANES // WIDTH)) + PAUSE
    early_sems = [piece[3] for piece in firsts]
    done = [block_at(i) for i in range(quarter, n // 2 - 2)]
    events = sorted(e for e in events if not (e[1] == 1 and e[2] in early_sems and e[3] in done))

    def advance(at, step, sem, q):
        finish(pieces[sem], step, q)
        if step < bits - 1 and q >= n >> (step + 2):
            copy_of(pieces[sem], step + 1, q).start()

    while events and events[0][0] <= begin:
        advance(*events.pop(0))

    sums = jnp.concatenate(
        [early[0, HALF : HALF + CLASSES, :], early[0, HALF + CLASSES : TOP, :]], axis=1
    )
    count_row = early[0, TOP : TOP + 1, 0:CLASSES]
    eye = iota((CLASSES, CLASSES), 0) == iota((CLASSES, CLASSES), 1)
    counts = jnp.sum(jnp.where(eye, count_row, 0.0), axis=1, keepdims=True)
    total = jnp.sum(counts, axis=0, keepdims=True)
    centers = jnp.sum(sums, axis=0, keepdims=True) / total
    scaled = sums / jnp.maximum(counts, 1.0)
    row, col = iota((LANES, LANES), 0), iota((LANES, LANES), 1)
    ridge = jnp.where(row == col, RIDGE, 0.0)
    diag = early[0, TOP + 1 : TOP + 2, :]
    between = exact(scaled, sums, TN)
    shifts = (sums - counts * centers) / total
    square = unpack(early[0, 0:HALF, :], pltpu.roll(jnp.broadcast_to(diag, (GROUP, LANES)), HALF, 1)[0:1, :])
    turn_over = lambda x: pltpu.roll(x, HALF, 1)
    system = (square - between[:LANES, :LANES]) / total + ridge
    rows = rows_of(system[:HALF, :])
    for turned in range(LANES // WIDTH):
        if turned == HALF // WIDTH:
            solved = jnp.concatenate(rows, axis=0)
            inner = -turn_over(solved)
            corner = turn_over(system[:HALF, :])[:, :HALF]
            rows = rows_of(turn_over(system[HALF:, :]) - exact(corner, inner, TN))
        while events and events[0][0] <= begin + STEP * turned:
            advance(*events.pop(0))
        rows = pivot(rows, WIDTH * turned % HALF, True)
    corner = jnp.concatenate(rows, axis=0)
    across = exact(corner[:, :HALF], inner[:, :HALF], NT)
    above = exact(inner[:, :HALF], corner[:, :HALF], NN)
    first = solved[:, :HALF] + exact(inner[:, :HALF], across, NN)
    inverse = jnp.concatenate(
        [
            jnp.concatenate([first, -above], axis=1),
            jnp.concatenate([-across, corner[:, :HALF]], axis=1),
        ],
        axis=0,
    )
    while events and events[0][0] <= arrive:
        advance(*events.pop(0))

    col = iota((LANES, LANES), 1)
    kept = col < HALF
    stack = lambda x: jnp.concatenate([x, turn_over(x)], axis=0)
    beside, below = between[:LANES, LANES:], between[LANES:, LANES:]
    last = (unpack(late[0, HALF:LANES, :], diag) - below) / total + ridge
    cross = jnp.where(kept, (stack(late[0, 0:HALF, :]) - beside) / total, 0.0)
    gain = exact(inverse, cross, NN)
    rows = rows_of(last[:HALF, :] - exact(cross[:, :HALF], gain, TN))
    far = shifts[:, LANES:] - exact(shifts[:, :LANES], gain, NN)
    left = exact(shifts[:, :LANES], inverse, NN)
    for turned in range(HALF // WIDTH):
        while events and events[0][0] <= resume + STEP * turned:
            advance(*events.pop(0))
        rows = pivot(rows, WIDTH * turned, True)
    for event in events:
        advance(*event)

    middle = jnp.concatenate(rows, axis=0)[:, :HALF]
    far = far[:, :HALF]
    near = exact(far, middle, NN)
    other = (stack(late[0, LANES:LATE, :]) - turn_over(beside)) / total
    other = jnp.where(kept, other, 0.0)
    pull = exact(inverse, other, NN)
    both = jnp.where(kept, cross, turn_over(other))
    rest = turn_over(last) - exact(both, pull, TN)
    side = rest[:HALF, :]
    link = exact(middle, side, NN)
    rows = rows_of(rest[HALF:, :] - exact(side[:, :HALF], link, TN))
    end = turn_over(shifts[:, LANES:]) - exact(shifts[:, :LANES], pull, NN) - exact(far, link, NN)
    rows = rows + rows_of(end)
    gains = jnp.where(kept, gain, turn_over(pull))
    for turned in range(HALF // WIDTH):
        rows = pivot(rows, WIDTH * turned, False)
    end = jnp.concatenate(rows[HALF // GROUP :], axis=0)[:, :HALF]
    right = jnp.concatenate([near - exact(end, link[:, :HALF], NT), end], axis=1)
    left = left - exact(right, gains, NT)
    planes = jnp.concatenate([left, right], axis=1)
    planes_ref[...] = planes
    offsets = -jnp.sum(planes * centers, axis=1, keepdims=True)
    mine[...] = planes.astype(jnp.bfloat16)
    mine_offsets[:, 0:CLASSES] = jnp.sum(jnp.where(eye, offsets, 0.0), axis=0, keepdims=True)

    def far_copy(r):
        return pltpu.make_async_remote_copy(
            src_ref=mine,
            dst_ref=messages.at[r],
            send_sem=far_send.at[r],
            recv_sem=far_recv.at[r],
            device_id={"rows": device_at(me, r)},
        )

    def offset_copy(r):
        return pltpu.make_async_remote_copy(
            src_ref=mine_offsets,
            dst_ref=message_offsets.at[r],
            send_sem=near_send.at[r],
            recv_sem=near_recv.at[r],
            device_id={"rows": device_at(me, r)},
        )

    def score(r):
        q = sum(((r >> b) % 2) << (bits - 1 - b) for b in range(bits))
        node = nodes_ref[q]
        message, offset_row = (mine, mine_offsets) if r == 0 else (messages.at[r], message_offsets.at[r])
        offsets = jnp.sum(jnp.where(eye, offset_row[:, 0:CLASSES], 0.0), axis=1, keepdims=True)
        values = lax.dot_general(message[...], x_ref[node], NT, preferred_element_type=jnp.float32)
        values = values + offsets
        ids = ids_ref[pl.ds(node * tiles, tiles), :]
        for k in range(tiles):
            part = values[:, k * LANES : (k + 1) * LANES]
            scores[r, :, k * LANES : (k + 1) * LANES] = jnp.where(ids[k : k + 1, :] == node, part, 0.0)

    turns = list(range(1, n))
    for r in reversed(turns):
        far_copy(r).start()
        offset_copy(r).start()
    score(0)
    for start in range(0, n, BATCH):
        batch = range(max(start, 1), start + BATCH)
        for r in batch:
            far_copy(r).wait_recv()
            offset_copy(r).wait_recv()
        for r in batch:
            score(r)
    for k in range(n):
        out_ref[:, k * seg : (k + 1) * seg] = scores[lax.bitwise_xor(owners_ref[k], me)]
    for step in range(bits):
        half = n >> (step + 1)
        for piece in pieces[2:] if step else wholes:
            for q in range(half, 2 * half):
                copy_of(piece, step, q).wait_send()
    for r in turns:
        far_copy(r).wait_send()
        offset_copy(r).wait_send()


def place_kernel(planes, scores, planes_out, scores_out, sems):
    copies = [
        pltpu.make_async_copy(scores, scores_out, sems.at[0]),
        pltpu.make_async_copy(planes, planes_out, sems.at[1]),
    ]
    for copy in copies:
        copy.start()
    for copy in copies:
        copy.wait()


def on_device(features, node_ids, labels, owners):
    row_count, feat = features.shape
    n = owners.shape[0]
    seg = row_count // n
    ids = node_ids.reshape(row_count // LANES, LANES)
    tags = labels.reshape(row_count // LANES, LANES)
    hbm = pl.BlockSpec(memory_space=pltpu.HBM)
    sems = len(EARLY_CUTS) + len(LATE_CUTS)
    whole = pl.BlockSpec(memory_space=pltpu.VMEM)
    dma = pltpu.SemaphoreType.DMA

    planes, scores = pl.pallas_call(
        functools.partial(tree_kernel, n),
        out_shape=(
            pltpu.VMEM((CLASSES, feat), jnp.float32),
            pltpu.VMEM((CLASSES, row_count), jnp.float32),
        ),
        in_specs=[hbm] * 4,
        out_specs=(whole, whole),
        scratch_shapes=[
            pltpu.SMEM((n,), jnp.int32),
            pltpu.SMEM((n,), jnp.int32),
            pltpu.VMEM((n, seg, feat), features.dtype),
            pltpu.VMEM(ids.shape, jnp.int32),
            pltpu.VMEM(ids.shape, jnp.int32),
            pltpu.VMEM((n, CLASSES, seg), jnp.bfloat16),
            pltpu.VMEM((n, GROUP, LANES), jnp.float32),
            pltpu.VMEM((n, EARLY, LANES), jnp.float32),
            pltpu.VMEM((n, EARLY, LANES), jnp.float32),
            pltpu.VMEM((n, LATE, LANES), jnp.float32),
            pltpu.VMEM((n, LATE, LANES), jnp.float32),
            pltpu.VMEM((CLASSES, feat), jnp.bfloat16),
            pltpu.VMEM((n, CLASSES, feat), jnp.bfloat16),
            pltpu.VMEM((1, LANES), jnp.float32),
            pltpu.VMEM((n, 1, LANES), jnp.float32),
            pltpu.VMEM((n, CLASSES, seg), jnp.float32),
            dma((3 + CHUNKS,)),
            dma((sems, n)),
            dma((sems, n)),
            dma((n,)),
            dma((n,)),
            dma((n,)),
            dma((n,)),
        ],
        compiler_params=pltpu.CompilerParams(
            collective_id=0, has_side_effects=True, vmem_limit_bytes=VMEM - 4 * CLASSES * (row_count + feat)
        ),
        name="tree",
    )(owners, features.reshape(n, seg, feat), ids, tags)

    planes, scores = pl.pallas_call(
        place_kernel,
        out_shape=(
            jax.ShapeDtypeStruct((CLASSES, feat), jnp.float32),
            jax.ShapeDtypeStruct((CLASSES, row_count), jnp.float32),
        ),
        in_specs=[whole, whole],
        out_specs=(hbm, hbm),
        scratch_shapes=[dma((2,))],
        name="place",
    )(*(pltpu.with_memory_space_constraint(x, pltpu.VMEM) for x in (planes, scores)))
    return planes[None], scores


def solution(mesh):
    in_specs = (P(("leaf", "rows"), None), P(("leaf", "rows")), P(("leaf", "rows")), P("leaf"))
    out_specs = (P(("leaf", "rows"), None, None), P(None, ("leaf", "rows")))
    return jax.shard_map(
        on_device, mesh=mesh, in_specs=in_specs, out_specs=out_specs, check_vma=False
    )
```

```python
import functools
import jax
import jax.numpy as jnp
from jax import lax
from jax.experimental import pallas as pl
from jax.experimental.pallas import tpu as pltpu
from jax.sharding import PartitionSpec as P

CLASSES = 16
LANES = 128
HALF = LANES // 2
GROUP = 8
WIDTH = 8
BATCH = 4
CHUNKS = 8
RIDGE = 0.1
HIGHEST = lax.Precision.HIGHEST
NN = (((1,), (0,)), ((), ()))
TN = (((0,), (0,)), ((), ()))
NT = (((1,), (1,)), ((), ()))
TOP = HALF + 2 * CLASSES
EARLY = TOP + GROUP
LATE = LANES + HALF
EARLY_CUTS = (0, EARLY)
LATE_CUTS = (0, LANES, LATE)
RATE, NEAR, FAR, STEP = 0.0085, 1.8, 2.6, 0.24
PAUSE, OPEN, TURN = 0.8, 4.0, 0.7
VMEM = 67043328


def iota(shape, dim):
    return lax.broadcasted_iota(jnp.int32, shape, dim)


def partner_of(me, bit):
    width = 1 << bit
    return me + width * (1 - 2 * ((me // width) % 2))


def device_at(me, r):
    bit = 0
    while r >> bit:
        if (r >> bit) % 2:
            me = partner_of(me, bit)
        bit += 1
    return me


def exact(a, b, dims):
    return lax.dot_general(a, b, dims, precision=HIGHEST, preferred_element_type=jnp.float32)


def pack(square):
    top, low = square[:HALF, :], square[HALF:, :]
    turned = pltpu.roll(low, HALF, 1)
    row, col = iota((HALF, LANES), 0), iota((HALF, LANES), 1)
    packed = jnp.where((row >= col) | (col >= HALF), top, turned)
    diag = jnp.sum(jnp.where(row + HALF == col, low, 0.0), axis=0, keepdims=True)
    return packed, diag


def unpack(packed, diag):
    row, col = iota((HALF, LANES), 0), iota((HALF, LANES), 1)
    turned = jnp.concatenate([packed, jnp.zeros_like(packed)], axis=0).T
    top = jnp.where((row >= col) | (col >= HALF), packed, turned[:HALF, :])
    last = jnp.where(row < col, packed, jnp.where(row == col, diag, turned[:HALF, :]))
    low = jnp.where(col < HALF, turned[HALF:, :], pltpu.roll(last, HALF, 1))
    return jnp.concatenate([top, low], axis=0)


def mark(node, ids_ref, labels_ref, hot_ref, tally_ref):
    seg = hot_ref.shape[2]
    tiles = seg // LANES
    tags = labels_ref[pl.ds(node * tiles, tiles), :]
    live = ids_ref[pl.ds(node * tiles, tiles), :] == node
    length = jnp.sum(live.astype(jnp.float32), axis=(0, 1), keepdims=True)
    tags = jnp.where(live, tags, -1)
    hot = jnp.concatenate(
        [tags[k : k + 1, :] == iota((CLASSES, LANES), 0) for k in range(tiles)], axis=1
    )
    hot = hot.astype(jnp.float32).astype(jnp.bfloat16)
    counts = lax.dot_general(
        jnp.ones((GROUP, seg), jnp.bfloat16), hot, NT, preferred_element_type=jnp.float32
    )
    counts = jnp.concatenate([counts, jnp.zeros((GROUP, LANES - CLASSES), jnp.float32)], axis=1)
    hot_ref[node] = hot
    tally_ref[node] = jnp.where(iota((GROUP, LANES), 0) == 0, counts, length)


def one_partial(node, q, x_ref, hot_ref, tally_ref, early, late):
    seg, feat = x_ref.shape[1:]
    tally = tally_ref[node]
    x = x_ref[node]
    position = iota((seg, feat), 0).astype(jnp.float32)
    length = jnp.concatenate([tally[1:2, :]] * (feat // LANES), axis=1)
    x = jnp.where(position < length, x, jnp.zeros((), x.dtype))
    moment = lax.dot_general(x, x, TN, preferred_element_type=jnp.float32)
    sums = jnp.dot(hot_ref[node], x, preferred_element_type=jnp.float32)
    packed, diag = pack(moment[:LANES, :LANES])
    early[q, 0:HALF, :] = packed
    early[q, HALF : HALF + CLASSES, :] = sums[:, :LANES]
    early[q, HALF + CLASSES : TOP, :] = sums[:, LANES:]
    packed, other = pack(moment[LANES:, LANES:])
    diag = diag + pltpu.roll(jnp.broadcast_to(other, (GROUP, LANES)), HALF, 1)
    early[q, TOP:EARLY, :] = jnp.where(iota((GROUP, LANES), 0) == 0, tally, diag)
    top, low = moment[:HALF, LANES:], moment[HALF:LANES, LANES:]
    left = iota((HALF, LANES), 1) < HALF
    late[q, 0:HALF, :] = jnp.where(left, top, pltpu.roll(low, HALF, 1))
    late[q, HALF:LANES, :] = packed
    late[q, LANES:LATE, :] = jnp.where(left, pltpu.roll(top, HALF, 1), low)


def lane_of(x, lane):
    return jnp.broadcast_to(x[:, lane : lane + 1], x.shape)


def dot(a, b):
    terms = [x * y for x, y in zip(a, b)]
    while len(terms) > 1:
        terms = [terms[k] + terms[k + 1] for k in range(0, len(terms), 2)]
    return terms[0]


def invert2(a, b, c):
    inv = 1.0 / (a * c - b * b)
    return c * inv, -b * inv, a * inv


def parts4(d):
    p00, p01, p11 = invert2(d[0][0], d[0][1], d[1][1])
    q = [[d[0][2], d[0][3]], [d[1][2], d[1][3]]]
    t = [
        [p00 * q[0][j] + p01 * q[1][j] for j in (0, 1)],
        [p01 * q[0][j] + p11 * q[1][j] for j in (0, 1)],
    ]
    s = lambda i, j: d[2 + i][2 + j] - (q[0][i] * t[0][j] + q[1][i] * t[1][j])
    h00, h01, h11 = invert2(s(0, 0), s(0, 1), s(1, 1))
    return p00, p01, p11, t, h00, h01, h11


def inverse4(d):
    p00, p01, p11, t, h00, h01, h11 = parts4(d)
    u = [[t[i][0] * h00 + t[i][1] * h01, t[i][0] * h01 + t[i][1] * h11] for i in (0, 1)]
    e = lambda p, i, j: p + (u[i][0] * t[j][0] + u[i][1] * t[j][1])
    e00, e01, e11 = e(p00, 0, 0), e(p01, 0, 1), e(p11, 1, 1)
    return [
        [e00, e01, -u[0][0], -u[0][1]],
        [e01, e11, -u[1][0], -u[1][1]],
        [-u[0][0], -u[1][0], h00, h01],
        [-u[0][1], -u[1][1], h01, h11],
    ]


def solve4(d, n):
    p00, p01, p11, t, h00, h01, h11 = parts4(d)
    m2 = n[2] - (t[0][0] * n[0] + t[1][0] * n[1])
    m3 = n[3] - (t[0][1] * n[0] + t[1][1] * n[1])
    w2, w3 = h00 * m2 + h01 * m3, h01 * m2 + h11 * m3
    w0 = (p00 * n[0] + p01 * n[1]) - (t[0][0] * w2 + t[0][1] * w3)
    w1 = (p01 * n[0] + p11 * n[1]) - (t[1][0] * w2 + t[1][1] * w3)
    return [w0, w1, w2, w3]


def solve8(d, n):
    four = range(4)
    p = inverse4([row[:4] for row in d[:4]])
    q = [row[4:] for row in d[:4]]
    t = [[dot(p[i], [q[k][j] for k in four]) for j in four] for i in four]
    s = [[None] * 4 for i in four]
    for i in four:
        for j in range(i, 4):
            s[i][j] = d[4 + i][4 + j] - dot([q[k][i] for k in four], [t[k][j] for k in four])
    m = [n[4 + i] - dot([t[k][i] for k in four], n[:4]) for i in four]
    low = solve4(s, m)
    return [dot(p[i], n[:4]) - dot(t[i], low) for i in four] + low


def pivot(rows, at, whole):
    group = at // GROUP
    shape = (GROUP, LANES)
    lanes, lane, depth = iota(shape, 1), iota((1, LANES), 1), iota(shape, 0)
    span = range(WIDTH)
    pivots = rows[group]
    spread = [lane_of(pivots, at + u) for u in span]
    d = [[spread[u][t : t + 1, :] if u >= t else None for u in span] for t in span]
    inside, within = (lanes >= at) & (lanes < at + WIDTH), (lane >= at) & (lane < at + WIDTH)
    near = [
        jnp.where(within, jnp.where(lane == at + t, -1.0, 0.0), pivots[t : t + 1, :]) for t in span
    ]
    w = [jnp.broadcast_to(x, shape) for x in solve8(d, near)]
    out = list(rows)
    if whole:
        own = w[0]
        for t in span:
            own = jnp.where(depth == t, w[t], own)
        out[group] = -own
    for g in range(0 if whole else group + 1, len(rows)):
        if g != group:
            k = [lane_of(rows[g], at + u) for u in span]
            out[g] = jnp.where(inside, 0.0, rows[g]) - dot(k, w)
    return out


def rows_of(x):
    return [x[g : g + GROUP, :] for g in range(0, x.shape[0], GROUP)]


def tree_kernel(
    n,
    owners_hbm,
    x_hbm,
    ids_hbm,
    labels_hbm,
    planes_ref,
    out_ref,
    owners_ref,
    nodes_ref,
    x_ref,
    ids_ref,
    labels_ref,
    hot_ref,
    tally_ref,
    early,
    early_in,
    late,
    late_in,
    mine,
    messages,
    mine_offsets,
    message_offsets,
    scores,
    load_sems,
    sum_send,
    sum_recv,
    far_send,
    far_recv,
    near_send,
    near_recv,
):
    bits = n.bit_length() - 1
    seg, feat = x_ref.shape[1:]
    tiles = seg // LANES
    me = lax.axis_index("rows")
    barrier = pltpu.get_barrier_semaphore()
    pairs = [(owners_hbm, owners_ref), (ids_hbm, ids_ref), (labels_hbm, labels_ref)]
    part = n // CHUNKS
    for k in range(CHUNKS):
        pairs.append((x_hbm.at[pl.ds(k * part, part)], x_ref.at[pl.ds(k * part, part)]))
    loads = [pltpu.make_async_copy(a, b, load_sems.at[k]) for k, (a, b) in enumerate(pairs)]
    for load in loads:
        load.start()
    for bit in range(bits):
        pl.semaphore_signal(barrier, inc=1, device_id={"rows": partner_of(me, bit)})
    for load in loads[:3]:
        load.wait()

    def prepare(k, carry):
        mark(k, ids_ref, labels_ref, hot_ref, tally_ref)
        return carry

    lax.fori_loop(0, n, prepare, 0, unroll=8)
    for load in loads[3:]:
        load.wait()
    pl.semaphore_wait(barrier, bits)

    wholes = [(0, 0, EARLY, 0), (1, 0, LATE, 1)]
    pieces = list(wholes)
    for part, cuts in enumerate((EARLY_CUTS, LATE_CUTS)):
        pieces += [(part, lo, hi - lo, len(pieces) + k) for k, (lo, hi) in enumerate(zip(cuts, cuts[1:]))]
    firsts = [p for p in pieces[2:] if p[0] == 0]
    middles = [p for p in pieces[2:] if p[0] == 1 and p[1] < LANES]
    lasts = [p for p in pieces[2:] if p[0] == 1 and p[1] >= LANES]
    held, landed = (early, late), (early_in, late_in)

    def copy_of(piece, step, q):
        part, low, size, sem = piece
        return pltpu.make_async_remote_copy(
            src_ref=held[part].at[q, pl.ds(low, size)],
            dst_ref=landed[part].at[q, pl.ds(low, size)],
            send_sem=sum_send.at[sem, q],
            recv_sem=sum_recv.at[sem, q],
            device_id={"rows": partner_of(me, step)},
        )

    def partial(q):
        slot = 0
        for b in range(bits):
            mine, theirs = (me // (1 << b)) % 2, (q // (1 << (bits - 1 - b))) % 2
            slot = slot + (1 << b) * ((mine + theirs) % 2)
        node = 0
        for k in range(n):
            node = jnp.where(owners_ref[k] == slot, k, node)
        nodes_ref[q] = node
        one_partial(node, q, x_ref, hot_ref, tally_ref, early, late)

    def finish(piece, step, q):
        half = n >> (step + 1)
        copy_of(piece, step, q + half).wait_recv()
        part, low, size, sem = piece
        rows = pl.ds(low, size)
        held[part][q, rows] = held[part][q, rows] + landed[part][q + half, rows]

    quarter = n // 4

    def turn(i):
        low = quarter - 1 - i % quarter
        for b in range(bits - 2):
            yield (low // (1 << b)) % 2, bits - 3 - b
        yield 1 - i // quarter, bits - 2

    def block_at(i):
        return sum(bit * (1 << place) for bit, place in turn(i))

    def pair(i, carry):
        q = block_at(i)
        partial(q + n // 2)
        partial(q)
        for piece in wholes:
            copy_of(piece, 0, q + n // 2).start()

        @pl.when(i >= 1)
        def _():
            before = block_at(i - 1)
            finish(wholes[0], 0, before)

            @pl.when(i - 1 < quarter)
            def _():
                for piece in firsts:
                    copy_of(piece, 1, before).start()

        @pl.when(i >= quarter + 2)
        def _():
            before = block_at(i - 2)
            for piece in firsts:
                finish(piece, 1, before)

            @pl.when(before >= n // 8)
            def _():
                for piece in firsts:
                    copy_of(piece, 2, before).start()

        @pl.when(i >= 1)
        def _():
            finish(wholes[1], 0, block_at(i - 1))

        @pl.when(i >= quarter + 1)
        def _():
            for piece in middles:
                copy_of(piece, 1, block_at(i - 1 - quarter)).start()

        return carry

    lax.fori_loop(0, n // 2, pair, 0)
    finish(wholes[0], 0, 0)
    for piece in middles:
        copy_of(piece, 1, block_at(quarter - 1)).start()
    for j in range(quarter):
        for piece in lasts:
            copy_of(piece, 1, block_at(j)).start()
    finish(wholes[1], 0, 0)

    free = [0.0] * bits
    queue = []

    def post(at, step, q, piece):
        begin = max(at, free[step])
        free[step] = begin + RATE * piece[2]
        queue.append((free[step] + (NEAR if step < bits - 1 else FAR), step, piece[3], q - (n >> (step + 1))))

    for part, group in enumerate((firsts, middles, lasts)):
        for j in range(quarter):
            for piece in group:
                post(OPEN + TURN * (j + quarter * part), 1, block_at(j), piece)
    over, events = {}, []
    while queue:
        queue.sort()
        at, step, sem, q = queue.pop(0)
        if step > 1:
            if (step - 1, sem, q) not in over:
                queue.append((queue[0][0] + 0.001, step, sem, q))
                continue
            at = max(at, over[step - 1, sem, q])
        over[step, sem, q] = at
        events.append((at, step, sem, q))
        if step < bits - 1 and q >= n >> (step + 2):
            post(at, step + 1, q, pieces[sem])
    begin = max(over[bits - 1, piece[3], 0] for piece in firsts)
    arrive = max(over[bits - 1, piece[3], 0] for piece in middles)
    resume = max(arrive, begin + STEP * (LANES // WIDTH)) + PAUSE
    early_sems = [piece[3] for piece in firsts]
    done = [block_at(i) for i in range(quarter, n // 2 - 2)]
    events = sorted(e for e in events if not (e[1] == 1 and e[2] in early_sems and e[3] in done))

    def advance(at, step, sem, q):
        finish(pieces[sem], step, q)
        if step < bits - 1 and q >= n >> (step + 2):
            copy_of(pieces[sem], step + 1, q).start()

    while events and events[0][0] <= begin:
        advance(*events.pop(0))

    sums = jnp.concatenate(
        [early[0, HALF : HALF + CLASSES, :], early[0, HALF + CLASSES : TOP, :]], axis=1
    )
    count_row = early[0, TOP : TOP + 1, 0:CLASSES]
    eye = iota((CLASSES, CLASSES), 0) == iota((CLASSES, CLASSES), 1)
    counts = jnp.sum(jnp.where(eye, count_row, 0.0), axis=1, keepdims=True)
    total = jnp.sum(counts, axis=0, keepdims=True)
    centers = jnp.sum(sums, axis=0, keepdims=True) / total
    scaled = sums / jnp.maximum(counts, 1.0)
    row, col = iota((LANES, LANES), 0), iota((LANES, LANES), 1)
    ridge = jnp.where(row == col, RIDGE, 0.0)
    diag = early[0, TOP + 1 : TOP + 2, :]
    between = exact(scaled, sums, TN)
    shifts = (sums - counts * centers) / total
    square = unpack(early[0, 0:HALF, :], pltpu.roll(jnp.broadcast_to(diag, (GROUP, LANES)), HALF, 1)[0:1, :])
    turn_over = lambda x: pltpu.roll(x, HALF, 1)
    system = (square - between[:LANES, :LANES]) / total + ridge
    rows = rows_of(system[:HALF, :])
    for turned in range(LANES // WIDTH):
        if turned == HALF // WIDTH:
            solved = jnp.concatenate(rows, axis=0)
            inner = -turn_over(solved)
            corner = turn_over(system[:HALF, :])[:, :HALF]
            rows = rows_of(turn_over(system[HALF:, :]) - exact(corner, inner, TN))
        while events and events[0][0] <= begin + STEP * turned:
            advance(*events.pop(0))
        rows = pivot(rows, WIDTH * turned % HALF, True)
    corner = jnp.concatenate(rows, axis=0)
    across = exact(corner[:, :HALF], inner[:, :HALF], NT)
    above = exact(inner[:, :HALF], corner[:, :HALF], NN)
    first = solved[:, :HALF] + exact(inner[:, :HALF], across, NN)
    inverse = jnp.concatenate(
        [
            jnp.concatenate([first, -above], axis=1),
            jnp.concatenate([-across, corner[:, :HALF]], axis=1),
        ],
        axis=0,
    )
    while events and events[0][0] <= arrive:
        advance(*events.pop(0))

    col = iota((LANES, LANES), 1)
    kept = col < HALF
    stack = lambda x: jnp.concatenate([x, turn_over(x)], axis=0)
    beside, below = between[:LANES, LANES:], between[LANES:, LANES:]
    last = (unpack(late[0, HALF:LANES, :], diag) - below) / total + ridge
    cross = jnp.where(kept, (stack(late[0, 0:HALF, :]) - beside) / total, 0.0)
    gain = exact(inverse, cross, NN)
    rows = rows_of(last[:HALF, :] - exact(cross[:, :HALF], gain, TN))
    far = shifts[:, LANES:] - exact(shifts[:, :LANES], gain, NN)
    left = exact(shifts[:, :LANES], inverse, NN)
    for turned in range(HALF // WIDTH):
        while events and events[0][0] <= resume + STEP * turned:
            advance(*events.pop(0))
        rows = pivot(rows, WIDTH * turned, True)
    for event in events:
        advance(*event)

    middle = jnp.concatenate(rows, axis=0)[:, :HALF]
    far = far[:, :HALF]
    near = exact(far, middle, NN)
    other = (stack(late[0, LANES:LATE, :]) - turn_over(beside)) / total
    other = jnp.where(kept, other, 0.0)
    pull = exact(inverse, other, NN)
    both = jnp.where(kept, cross, turn_over(other))
    rest = turn_over(last) - exact(both, pull, TN)
    side = rest[:HALF, :]
    link = exact(middle, side, NN)
    rows = rows_of(rest[HALF:, :] - exact(side[:, :HALF], link, TN))
    end = turn_over(shifts[:, LANES:]) - exact(shifts[:, :LANES], pull, NN) - exact(far, link, NN)
    rows = rows + rows_of(end)
    gains = jnp.where(kept, gain, turn_over(pull))
    for turned in range(HALF // WIDTH):
        rows = pivot(rows, WIDTH * turned, False)
    end = jnp.concatenate(rows[HALF // GROUP :], axis=0)[:, :HALF]
    right = jnp.concatenate([near - exact(end, link[:, :HALF], NT), end], axis=1)
    left = left - exact(right, gains, NT)
    planes = jnp.concatenate([left, right], axis=1)
    planes_ref[...] = planes
    offsets = -jnp.sum(planes * centers, axis=1, keepdims=True)
    mine[...] = planes.astype(jnp.bfloat16)
    mine_offsets[:, 0:CLASSES] = jnp.sum(jnp.where(eye, offsets, 0.0), axis=0, keepdims=True)

    def far_copy(r):
        return pltpu.make_async_remote_copy(
            src_ref=mine,
            dst_ref=messages.at[r],
            send_sem=far_send.at[r],
            recv_sem=far_recv.at[r],
            device_id={"rows": device_at(me, r)},
        )

    def offset_copy(r):
        return pltpu.make_async_remote_copy(
            src_ref=mine_offsets,
            dst_ref=message_offsets.at[r],
            send_sem=near_send.at[r],
            recv_sem=near_recv.at[r],
            device_id={"rows": device_at(me, r)},
        )

    def score(r):
        q = sum(((r >> b) % 2) << (bits - 1 - b) for b in range(bits))
        node = nodes_ref[q]
        message, offset_row = (mine, mine_offsets) if r == 0 else (messages.at[r], message_offsets.at[r])
        offsets = jnp.sum(jnp.where(eye, offset_row[:, 0:CLASSES], 0.0), axis=1, keepdims=True)
        values = lax.dot_general(message[...], x_ref[node], NT, preferred_element_type=jnp.float32)
        values = values + offsets
        ids = ids_ref[pl.ds(node * tiles, tiles), :]
        for k in range(tiles):
            part = values[:, k * LANES : (k + 1) * LANES]
            scores[r, :, k * LANES : (k + 1) * LANES] = jnp.where(ids[k : k + 1, :] == node, part, 0.0)

    turns = list(range(1, n))
    for r in reversed(turns):
        far_copy(r).start()
        offset_copy(r).start()
    score(0)
    for start in range(0, n, BATCH):
        batch = range(max(start, 1), start + BATCH)
        for r in batch:
            far_copy(r).wait_recv()
            offset_copy(r).wait_recv()
        for r in batch:
            score(r)
    for k in range(n):
        out_ref[:, k * seg : (k + 1) * seg] = scores[lax.bitwise_xor(owners_ref[k], me)]
    for step in range(bits):
        half = n >> (step + 1)
        for piece in pieces[2:] if step else wholes:
            for q in range(half, 2 * half):
                copy_of(piece, step, q).wait_send()
    for r in turns:
        far_copy(r).wait_send()
        offset_copy(r).wait_send()


def place_kernel(planes, scores, planes_out, scores_out, sems):
    copies = [
        pltpu.make_async_copy(scores, scores_out, sems.at[0]),
        pltpu.make_async_copy(planes, planes_out, sems.at[1]),
    ]
    for copy in copies:
        copy.start()
    for copy in copies:
        copy.wait()


def on_device(features, node_ids, labels, owners):
    row_count, feat = features.shape
    n = owners.shape[0]
    seg = row_count // n
    ids = node_ids.reshape(row_count // LANES, LANES)
    tags = labels.reshape(row_count // LANES, LANES)
    hbm = pl.BlockSpec(memory_space=pltpu.HBM)
    sems = len(EARLY_CUTS) + len(LATE_CUTS)
    whole = pl.BlockSpec(memory_space=pltpu.VMEM)
    dma = pltpu.SemaphoreType.DMA

    planes, scores = pl.pallas_call(
        functools.partial(tree_kernel, n),
        out_shape=(
            pltpu.VMEM((CLASSES, feat), jnp.float32),
            pltpu.VMEM((CLASSES, row_count), jnp.float32),
        ),
        in_specs=[hbm] * 4,
        out_specs=(whole, whole),
        scratch_shapes=[
            pltpu.SMEM((n,), jnp.int32),
            pltpu.SMEM((n,), jnp.int32),
            pltpu.VMEM((n, seg, feat), features.dtype),
            pltpu.VMEM(ids.shape, jnp.int32),
            pltpu.VMEM(ids.shape, jnp.int32),
            pltpu.VMEM((n, CLASSES, seg), jnp.bfloat16),
            pltpu.VMEM((n, GROUP, LANES), jnp.float32),
            pltpu.VMEM((n, EARLY, LANES), jnp.float32),
            pltpu.VMEM((n, EARLY, LANES), jnp.float32),
            pltpu.VMEM((n, LATE, LANES), jnp.float32),
            pltpu.VMEM((n, LATE, LANES), jnp.float32),
            pltpu.VMEM((CLASSES, feat), jnp.bfloat16),
            pltpu.VMEM((n, CLASSES, feat), jnp.bfloat16),
            pltpu.VMEM((1, LANES), jnp.float32),
            pltpu.VMEM((n, 1, LANES), jnp.float32),
            pltpu.VMEM((n, CLASSES, seg), jnp.float32),
            dma((3 + CHUNKS,)),
            dma((sems, n)),
            dma((sems, n)),
            dma((n,)),
            dma((n,)),
            dma((n,)),
            dma((n,)),
        ],
        compiler_params=pltpu.CompilerParams(
            collective_id=0, has_side_effects=True, vmem_limit_bytes=VMEM - 4 * CLASSES * (row_count + feat)
        ),
        name="tree",
    )(owners, features.reshape(n, seg, feat), ids, tags)

    planes, scores = pl.pallas_call(
        place_kernel,
        out_shape=(
            jax.ShapeDtypeStruct((CLASSES, feat), jnp.float32),
            jax.ShapeDtypeStruct((CLASSES, row_count), jnp.float32),
        ),
        in_specs=[whole, whole],
        out_specs=(hbm, hbm),
        scratch_shapes=[dma((2,))],
        name="place",
    )(*(pltpu.with_memory_space_constraint(x, pltpu.VMEM) for x in (planes, scores)))
    return planes[None], scores


def solution(mesh):
    in_specs = (P(("leaf", "rows"), None), P(("leaf", "rows")), P(("leaf", "rows")), P("leaf"))
    out_specs = (P(("leaf", "rows"), None, None), P(None, ("leaf", "rows")))
    return jax.shard_map(
        on_device, mesh=mesh, in_specs=in_specs, out_specs=out_specs, check_vma=False
    )
```

```python
import functools
import jax
import jax.numpy as jnp
from jax import lax
from jax.experimental import pallas as pl
from jax.experimental.pallas import tpu as pltpu
from jax.sharding import PartitionSpec as P

CLASSES = 16
LANES = 128
HALF = LANES // 2
GROUP = 8
WIDTH = 8
BATCH = 2
CHUNKS = 8
RIDGE = 0.1
HIGHEST = lax.Precision.HIGHEST
NN = (((1,), (0,)), ((), ()))
TN = (((0,), (0,)), ((), ()))
NT = (((1,), (1,)), ((), ()))
TOP = HALF + 2 * CLASSES
EARLY = TOP + GROUP
LATE = LANES + HALF
EARLY_CUTS = (0, EARLY)
LATE_CUTS = (0, LANES, LATE)
RATE, NEAR, FAR, STEP = 0.0085, 1.8, 2.6, 0.24
PAUSE, OPEN, TURN = 0.8, 4.0, 0.7
VMEM = 67043328


def iota(shape, dim):
    return lax.broadcasted_iota(jnp.int32, shape, dim)


def partner_of(me, bit):
    width = 1 << bit
    return me + width * (1 - 2 * ((me // width) % 2))


def device_at(me, r):
    bit = 0
    while r >> bit:
        if (r >> bit) % 2:
            me = partner_of(me, bit)
        bit += 1
    return me


def exact(a, b, dims):
    return lax.dot_general(a, b, dims, precision=HIGHEST, preferred_element_type=jnp.float32)


def pack(square):
    top, low = square[:HALF, :], square[HALF:, :]
    turned = pltpu.roll(low, HALF, 1)
    row, col = iota((HALF, LANES), 0), iota((HALF, LANES), 1)
    packed = jnp.where((row >= col) | (col >= HALF), top, turned)
    diag = jnp.sum(jnp.where(row + HALF == col, low, 0.0), axis=0, keepdims=True)
    return packed, diag


def unpack(packed, diag):
    row, col = iota((HALF, LANES), 0), iota((HALF, LANES), 1)
    turned = jnp.concatenate([packed, jnp.zeros_like(packed)], axis=0).T
    top = jnp.where((row >= col) | (col >= HALF), packed, turned[:HALF, :])
    last = jnp.where(row < col, packed, jnp.where(row == col, diag, turned[:HALF, :]))
    low = jnp.where(col < HALF, turned[HALF:, :], pltpu.roll(last, HALF, 1))
    return jnp.concatenate([top, low], axis=0)


def mark(node, ids_ref, labels_ref, hot_ref, tally_ref):
    seg = hot_ref.shape[2]
    tiles = seg // LANES
    tags = labels_ref[pl.ds(node * tiles, tiles), :]
    live = ids_ref[pl.ds(node * tiles, tiles), :] == node
    length = jnp.sum(live.astype(jnp.float32), axis=(0, 1), keepdims=True)
    tags = jnp.where(live, tags, -1)
    hot = jnp.concatenate(
        [tags[k : k + 1, :] == iota((CLASSES, LANES), 0) for k in range(tiles)], axis=1
    )
    hot = hot.astype(jnp.float32).astype(jnp.bfloat16)
    counts = lax.dot_general(
        jnp.ones((GROUP, seg), jnp.bfloat16), hot, NT, preferred_element_type=jnp.float32
    )
    counts = jnp.concatenate([counts, jnp.zeros((GROUP, LANES - CLASSES), jnp.float32)], axis=1)
    hot_ref[node] = hot
    tally_ref[node] = jnp.where(iota((GROUP, LANES), 0) == 0, counts, length)


def one_partial(node, q, x_ref, hot_ref, tally_ref, early, late):
    seg, feat = x_ref.shape[1:]
    tally = tally_ref[node]
    x = x_ref[node]
    position = iota((seg, feat), 0).astype(jnp.float32)
    length = jnp.concatenate([tally[1:2, :]] * (feat // LANES), axis=1)
    x = jnp.where(position < length, x, jnp.zeros((), x.dtype))
    moment = lax.dot_general(x, x, TN, preferred_element_type=jnp.float32)
    sums = jnp.dot(hot_ref[node], x, preferred_element_type=jnp.float32)
    packed, diag = pack(moment[:LANES, :LANES])
    early[q, 0:HALF, :] = packed
    early[q, HALF : HALF + CLASSES, :] = sums[:, :LANES]
    early[q, HALF + CLASSES : TOP, :] = sums[:, LANES:]
    packed, other = pack(moment[LANES:, LANES:])
    diag = diag + pltpu.roll(jnp.broadcast_to(other, (GROUP, LANES)), HALF, 1)
    early[q, TOP:EARLY, :] = jnp.where(iota((GROUP, LANES), 0) == 0, tally, diag)
    top, low = moment[:HALF, LANES:], moment[HALF:LANES, LANES:]
    left = iota((HALF, LANES), 1) < HALF
    late[q, 0:HALF, :] = jnp.where(left, top, pltpu.roll(low, HALF, 1))
    late[q, HALF:LANES, :] = packed
    late[q, LANES:LATE, :] = jnp.where(left, pltpu.roll(top, HALF, 1), low)


def lane_of(x, lane):
    return jnp.broadcast_to(x[:, lane : lane + 1], x.shape)


def dot(a, b):
    terms = [x * y for x, y in zip(a, b)]
    while len(terms) > 1:
        terms = [terms[k] + terms[k + 1] for k in range(0, len(terms), 2)]
    return terms[0]


def invert2(a, b, c):
    inv = 1.0 / (a * c - b * b)
    return c * inv, -b * inv, a * inv


def parts4(d):
    p00, p01, p11 = invert2(d[0][0], d[0][1], d[1][1])
    q = [[d[0][2], d[0][3]], [d[1][2], d[1][3]]]
    t = [
        [p00 * q[0][j] + p01 * q[1][j] for j in (0, 1)],
        [p01 * q[0][j] + p11 * q[1][j] for j in (0, 1)],
    ]
    s = lambda i, j: d[2 + i][2 + j] - (q[0][i] * t[0][j] + q[1][i] * t[1][j])
    h00, h01, h11 = invert2(s(0, 0), s(0, 1), s(1, 1))
    return p00, p01, p11, t, h00, h01, h11


def inverse4(d):
    p00, p01, p11, t, h00, h01, h11 = parts4(d)
    u = [[t[i][0] * h00 + t[i][1] * h01, t[i][0] * h01 + t[i][1] * h11] for i in (0, 1)]
    e = lambda p, i, j: p + (u[i][0] * t[j][0] + u[i][1] * t[j][1])
    e00, e01, e11 = e(p00, 0, 0), e(p01, 0, 1), e(p11, 1, 1)
    return [
        [e00, e01, -u[0][0], -u[0][1]],
        [e01, e11, -u[1][0], -u[1][1]],
        [-u[0][0], -u[1][0], h00, h01],
        [-u[0][1], -u[1][1], h01, h11],
    ]


def solve4(d, n):
    p00, p01, p11, t, h00, h01, h11 = parts4(d)
    m2 = n[2] - (t[0][0] * n[0] + t[1][0] * n[1])
    m3 = n[3] - (t[0][1] * n[0] + t[1][1] * n[1])
    w2, w3 = h00 * m2 + h01 * m3, h01 * m2 + h11 * m3
    w0 = (p00 * n[0] + p01 * n[1]) - (t[0][0] * w2 + t[0][1] * w3)
    w1 = (p01 * n[0] + p11 * n[1]) - (t[1][0] * w2 + t[1][1] * w3)
    return [w0, w1, w2, w3]


def solve8(d, n):
    four = range(4)
    p = inverse4([row[:4] for row in d[:4]])
    q = [row[4:] for row in d[:4]]
    t = [[dot(p[i], [q[k][j] for k in four]) for j in four] for i in four]
    s = [[None] * 4 for i in four]
    for i in four:
        for j in range(i, 4):
            s[i][j] = d[4 + i][4 + j] - dot([q[k][i] for k in four], [t[k][j] for k in four])
    m = [n[4 + i] - dot([t[k][i] for k in four], n[:4]) for i in four]
    low = solve4(s, m)
    return [dot(p[i], n[:4]) - dot(t[i], low) for i in four] + low


def pivot(rows, at, whole):
    group = at // GROUP
    shape = (GROUP, LANES)
    lanes, lane, depth = iota(shape, 1), iota((1, LANES), 1), iota(shape, 0)
    span = range(WIDTH)
    pivots = rows[group]
    spread = [lane_of(pivots, at + u) for u in span]
    d = [[spread[u][t : t + 1, :] if u >= t else None for u in span] for t in span]
    inside, within = (lanes >= at) & (lanes < at + WIDTH), (lane >= at) & (lane < at + WIDTH)
    near = [
        jnp.where(within, jnp.where(lane == at + t, -1.0, 0.0), pivots[t : t + 1, :]) for t in span
    ]
    w = [jnp.broadcast_to(x, shape) for x in solve8(d, near)]
    out = list(rows)
    if whole:
        own = w[0]
        for t in span:
            own = jnp.where(depth == t, w[t], own)
        out[group] = -own
    for g in range(0 if whole else group + 1, len(rows)):
        if g != group:
            k = [lane_of(rows[g], at + u) for u in span]
            out[g] = jnp.where(inside, 0.0, rows[g]) - dot(k, w)
    return out


def rows_of(x):
    return [x[g : g + GROUP, :] for g in range(0, x.shape[0], GROUP)]


def tree_kernel(
    n,
    owners_hbm,
    x_hbm,
    ids_hbm,
    labels_hbm,
    planes_ref,
    out_ref,
    owners_ref,
    nodes_ref,
    x_ref,
    ids_ref,
    labels_ref,
    hot_ref,
    tally_ref,
    early,
    early_in,
    late,
    late_in,
    mine,
    messages,
    mine_offsets,
    message_offsets,
    scores,
    load_sems,
    sum_send,
    sum_recv,
    far_send,
    far_recv,
    near_send,
    near_recv,
):
    bits = n.bit_length() - 1
    seg, feat = x_ref.shape[1:]
    tiles = seg // LANES
    me = lax.axis_index("rows")
    barrier = pltpu.get_barrier_semaphore()
    pairs = [(owners_hbm, owners_ref), (ids_hbm, ids_ref), (labels_hbm, labels_ref)]
    part = n // CHUNKS
    for k in range(CHUNKS):
        pairs.append((x_hbm.at[pl.ds(k * part, part)], x_ref.at[pl.ds(k * part, part)]))
    loads = [pltpu.make_async_copy(a, b, load_sems.at[k]) for k, (a, b) in enumerate(pairs)]
    for load in loads:
        load.start()
    for bit in range(bits):
        pl.semaphore_signal(barrier, inc=1, device_id={"rows": partner_of(me, bit)})
    for load in loads[:3]:
        load.wait()

    def prepare(k, carry):
        mark(k, ids_ref, labels_ref, hot_ref, tally_ref)
        return carry

    lax.fori_loop(0, n, prepare, 0, unroll=8)
    for load in loads[3:]:
        load.wait()
    pl.semaphore_wait(barrier, bits)

    wholes = [(0, 0, EARLY, 0), (1, 0, LATE, 1)]
    pieces = list(wholes)
    for part, cuts in enumerate((EARLY_CUTS, LATE_CUTS)):
        pieces += [(part, lo, hi - lo, len(pieces) + k) for k, (lo, hi) in enumerate(zip(cuts, cuts[1:]))]
    firsts = [p for p in pieces[2:] if p[0] == 0]
    middles = [p for p in pieces[2:] if p[0] == 1 and p[1] < LANES]
    lasts = [p for p in pieces[2:] if p[0] == 1 and p[1] >= LANES]
    held, landed = (early, late), (early_in, late_in)

    def copy_of(piece, step, q):
        part, low, size, sem = piece
        return pltpu.make_async_remote_copy(
            src_ref=held[part].at[q, pl.ds(low, size)],
            dst_ref=landed[part].at[q, pl.ds(low, size)],
            send_sem=sum_send.at[sem, q],
            recv_sem=sum_recv.at[sem, q],
            device_id={"rows": partner_of(me, step)},
        )

    def partial(q):
        slot = 0
        for b in range(bits):
            mine, theirs = (me // (1 << b)) % 2, (q // (1 << (bits - 1 - b))) % 2
            slot = slot + (1 << b) * ((mine + theirs) % 2)
        node = 0
        for k in range(n):
            node = jnp.where(owners_ref[k] == slot, k, node)
        nodes_ref[q] = node
        one_partial(node, q, x_ref, hot_ref, tally_ref, early, late)

    def finish(piece, step, q):
        half = n >> (step + 1)
        copy_of(piece, step, q + half).wait_recv()
        part, low, size, sem = piece
        rows = pl.ds(low, size)
        held[part][q, rows] = held[part][q, rows] + landed[part][q + half, rows]

    quarter = n // 4

    def turn(i):
        low = quarter - 1 - i % quarter
        for b in range(bits - 2):
            yield (low // (1 << b)) % 2, bits - 3 - b
        yield 1 - i // quarter, bits - 2

    def block_at(i):
        return sum(bit * (1 << place) for bit, place in turn(i))

    def pair(i, carry):
        q = block_at(i)
        partial(q + n // 2)
        partial(q)
        for piece in wholes:
            copy_of(piece, 0, q + n // 2).start()

        @pl.when(i >= 1)
        def _():
            before = block_at(i - 1)
            finish(wholes[0], 0, before)

            @pl.when(i - 1 < quarter)
            def _():
                for piece in firsts:
                    copy_of(piece, 1, before).start()

        @pl.when(i >= quarter + 2)
        def _():
            before = block_at(i - 2)
            for piece in firsts:
                finish(piece, 1, before)

            @pl.when(before >= n // 8)
            def _():
                for piece in firsts:
                    copy_of(piece, 2, before).start()

        @pl.when(i >= 1)
        def _():
            finish(wholes[1], 0, block_at(i - 1))

        @pl.when(i >= quarter + 1)
        def _():
            for piece in middles:
                copy_of(piece, 1, block_at(i - 1 - quarter)).start()

        return carry

    lax.fori_loop(0, n // 2, pair, 0)
    finish(wholes[0], 0, 0)
    for piece in middles:
        copy_of(piece, 1, block_at(quarter - 1)).start()
    for j in range(quarter):
        for piece in lasts:
            copy_of(piece, 1, block_at(j)).start()
    finish(wholes[1], 0, 0)

    free = [0.0] * bits
    queue = []

    def post(at, step, q, piece):
        begin = max(at, free[step])
        free[step] = begin + RATE * piece[2]
        queue.append((free[step] + (NEAR if step < bits - 1 else FAR), step, piece[3], q - (n >> (step + 1))))

    for part, group in enumerate((firsts, middles, lasts)):
        for j in range(quarter):
            for piece in group:
                post(OPEN + TURN * (j + quarter * part), 1, block_at(j), piece)
    over, events = {}, []
    while queue:
        queue.sort()
        at, step, sem, q = queue.pop(0)
        if step > 1:
            if (step - 1, sem, q) not in over:
                queue.append((queue[0][0] + 0.001, step, sem, q))
                continue
            at = max(at, over[step - 1, sem, q])
        over[step, sem, q] = at
        events.append((at, step, sem, q))
        if step < bits - 1 and q >= n >> (step + 2):
            post(at, step + 1, q, pieces[sem])
    begin = max(over[bits - 1, piece[3], 0] for piece in firsts)
    arrive = max(over[bits - 1, piece[3], 0] for piece in middles)
    resume = max(arrive, begin + STEP * (LANES // WIDTH)) + PAUSE
    early_sems = [piece[3] for piece in firsts]
    done = [block_at(i) for i in range(quarter, n // 2 - 2)]
    events = sorted(e for e in events if not (e[1] == 1 and e[2] in early_sems and e[3] in done))

    def advance(at, step, sem, q):
        finish(pieces[sem], step, q)
        if step < bits - 1 and q >= n >> (step + 2):
            copy_of(pieces[sem], step + 1, q).start()

    while events and events[0][0] <= begin:
        advance(*events.pop(0))

    sums = jnp.concatenate(
        [early[0, HALF : HALF + CLASSES, :], early[0, HALF + CLASSES : TOP, :]], axis=1
    )
    count_row = early[0, TOP : TOP + 1, 0:CLASSES]
    eye = iota((CLASSES, CLASSES), 0) == iota((CLASSES, CLASSES), 1)
    counts = jnp.sum(jnp.where(eye, count_row, 0.0), axis=1, keepdims=True)
    total = jnp.sum(counts, axis=0, keepdims=True)
    centers = jnp.sum(sums, axis=0, keepdims=True) / total
    scaled = sums / jnp.maximum(counts, 1.0)
    row, col = iota((LANES, LANES), 0), iota((LANES, LANES), 1)
    ridge = jnp.where(row == col, RIDGE, 0.0)
    diag = early[0, TOP + 1 : TOP + 2, :]
    between = exact(scaled, sums, TN)
    shifts = (sums - counts * centers) / total
    square = unpack(early[0, 0:HALF, :], pltpu.roll(jnp.broadcast_to(diag, (GROUP, LANES)), HALF, 1)[0:1, :])
    turn_over = lambda x: pltpu.roll(x, HALF, 1)
    system = (square - between[:LANES, :LANES]) / total + ridge
    rows = rows_of(system[:HALF, :])
    for turned in range(LANES // WIDTH):
        if turned == HALF // WIDTH:
            solved = jnp.concatenate(rows, axis=0)
            inner = -turn_over(solved)
            corner = turn_over(system[:HALF, :])[:, :HALF]
            rows = rows_of(turn_over(system[HALF:, :]) - exact(corner, inner, TN))
        while events and events[0][0] <= begin + STEP * turned:
            advance(*events.pop(0))
        rows = pivot(rows, WIDTH * turned % HALF, True)
    corner = jnp.concatenate(rows, axis=0)
    across = exact(corner[:, :HALF], inner[:, :HALF], NT)
    above = exact(inner[:, :HALF], corner[:, :HALF], NN)
    first = solved[:, :HALF] + exact(inner[:, :HALF], across, NN)
    inverse = jnp.concatenate(
        [
            jnp.concatenate([first, -above], axis=1),
            jnp.concatenate([-across, corner[:, :HALF]], axis=1),
        ],
        axis=0,
    )
    while events and events[0][0] <= arrive:
        advance(*events.pop(0))

    col = iota((LANES, LANES), 1)
    kept = col < HALF
    stack = lambda x: jnp.concatenate([x, turn_over(x)], axis=0)
    beside, below = between[:LANES, LANES:], between[LANES:, LANES:]
    last = (unpack(late[0, HALF:LANES, :], diag) - below) / total + ridge
    cross = jnp.where(kept, (stack(late[0, 0:HALF, :]) - beside) / total, 0.0)
    gain = exact(inverse, cross, NN)
    rows = rows_of(last[:HALF, :] - exact(cross[:, :HALF], gain, TN))
    far = shifts[:, LANES:] - exact(shifts[:, :LANES], gain, NN)
    left = exact(shifts[:, :LANES], inverse, NN)
    for turned in range(HALF // WIDTH):
        while events and events[0][0] <= resume + STEP * turned:
            advance(*events.pop(0))
        rows = pivot(rows, WIDTH * turned, True)
    for event in events:
        advance(*event)

    middle = jnp.concatenate(rows, axis=0)[:, :HALF]
    far = far[:, :HALF]
    near = exact(far, middle, NN)
    other = (stack(late[0, LANES:LATE, :]) - turn_over(beside)) / total
    other = jnp.where(kept, other, 0.0)
    pull = exact(inverse, other, NN)
    both = jnp.where(kept, cross, turn_over(other))
    rest = turn_over(last) - exact(both, pull, TN)
    side = rest[:HALF, :]
    link = exact(middle, side, NN)
    rows = rows_of(rest[HALF:, :] - exact(side[:, :HALF], link, TN))
    end = turn_over(shifts[:, LANES:]) - exact(shifts[:, :LANES], pull, NN) - exact(far, link, NN)
    rows = rows + rows_of(end)
    gains = jnp.where(kept, gain, turn_over(pull))
    for turned in range(HALF // WIDTH):
        rows = pivot(rows, WIDTH * turned, False)
    end = jnp.concatenate(rows[HALF // GROUP :], axis=0)[:, :HALF]
    right = jnp.concatenate([near - exact(end, link[:, :HALF], NT), end], axis=1)
    left = left - exact(right, gains, NT)
    planes = jnp.concatenate([left, right], axis=1)
    planes_ref[...] = planes
    offsets = -jnp.sum(planes * centers, axis=1, keepdims=True)
    mine[...] = planes.astype(jnp.bfloat16)
    mine_offsets[:, 0:CLASSES] = jnp.sum(jnp.where(eye, offsets, 0.0), axis=0, keepdims=True)

    def far_copy(r):
        return pltpu.make_async_remote_copy(
            src_ref=mine,
            dst_ref=messages.at[r],
            send_sem=far_send.at[r],
            recv_sem=far_recv.at[r],
            device_id={"rows": device_at(me, r)},
        )

    def offset_copy(r):
        return pltpu.make_async_remote_copy(
            src_ref=mine_offsets,
            dst_ref=message_offsets.at[r],
            send_sem=near_send.at[r],
            recv_sem=near_recv.at[r],
            device_id={"rows": device_at(me, r)},
        )

    def score(r):
        q = sum(((r >> b) % 2) << (bits - 1 - b) for b in range(bits))
        node = nodes_ref[q]
        message, offset_row = (mine, mine_offsets) if r == 0 else (messages.at[r], message_offsets.at[r])
        offsets = jnp.sum(jnp.where(eye, offset_row[:, 0:CLASSES], 0.0), axis=1, keepdims=True)
        values = lax.dot_general(message[...], x_ref[node], NT, preferred_element_type=jnp.float32)
        values = values + offsets
        ids = ids_ref[pl.ds(node * tiles, tiles), :]
        for k in range(tiles):
            part = values[:, k * LANES : (k + 1) * LANES]
            scores[r, :, k * LANES : (k + 1) * LANES] = jnp.where(ids[k : k + 1, :] == node, part, 0.0)

    turns = list(range(1, n))
    for r in reversed(turns):
        far_copy(r).start()
        offset_copy(r).start()
    score(0)
    for start in range(0, n, BATCH):
        batch = range(max(start, 1), start + BATCH)
        for r in batch:
            far_copy(r).wait_recv()
            offset_copy(r).wait_recv()
        for r in batch:
            score(r)
    for k in range(n):
        out_ref[:, k * seg : (k + 1) * seg] = scores[lax.bitwise_xor(owners_ref[k], me)]
    for step in range(bits):
        half = n >> (step + 1)
        for piece in pieces[2:] if step else wholes:
            for q in range(half, 2 * half):
                copy_of(piece, step, q).wait_send()
    for r in turns:
        far_copy(r).wait_send()
        offset_copy(r).wait_send()


def place_kernel(planes, scores, planes_out, scores_out, sems):
    copies = [
        pltpu.make_async_copy(scores, scores_out, sems.at[0]),
        pltpu.make_async_copy(planes, planes_out, sems.at[1]),
    ]
    for copy in copies:
        copy.start()
    for copy in copies:
        copy.wait()


def on_device(features, node_ids, labels, owners):
    row_count, feat = features.shape
    n = owners.shape[0]
    seg = row_count // n
    ids = node_ids.reshape(row_count // LANES, LANES)
    tags = labels.reshape(row_count // LANES, LANES)
    hbm = pl.BlockSpec(memory_space=pltpu.HBM)
    sems = len(EARLY_CUTS) + len(LATE_CUTS)
    whole = pl.BlockSpec(memory_space=pltpu.VMEM)
    dma = pltpu.SemaphoreType.DMA

    planes, scores = pl.pallas_call(
        functools.partial(tree_kernel, n),
        out_shape=(
            pltpu.VMEM((CLASSES, feat), jnp.float32),
            pltpu.VMEM((CLASSES, row_count), jnp.float32),
        ),
        in_specs=[hbm] * 4,
        out_specs=(whole, whole),
        scratch_shapes=[
            pltpu.SMEM((n,), jnp.int32),
            pltpu.SMEM((n,), jnp.int32),
            pltpu.VMEM((n, seg, feat), features.dtype),
            pltpu.VMEM(ids.shape, jnp.int32),
            pltpu.VMEM(ids.shape, jnp.int32),
            pltpu.VMEM((n, CLASSES, seg), jnp.bfloat16),
            pltpu.VMEM((n, GROUP, LANES), jnp.float32),
            pltpu.VMEM((n, EARLY, LANES), jnp.float32),
            pltpu.VMEM((n, EARLY, LANES), jnp.float32),
            pltpu.VMEM((n, LATE, LANES), jnp.float32),
            pltpu.VMEM((n, LATE, LANES), jnp.float32),
            pltpu.VMEM((CLASSES, feat), jnp.bfloat16),
            pltpu.VMEM((n, CLASSES, feat), jnp.bfloat16),
            pltpu.VMEM((1, LANES), jnp.float32),
            pltpu.VMEM((n, 1, LANES), jnp.float32),
            pltpu.VMEM((n, CLASSES, seg), jnp.float32),
            dma((3 + CHUNKS,)),
            dma((sems, n)),
            dma((sems, n)),
            dma((n,)),
            dma((n,)),
            dma((n,)),
            dma((n,)),
        ],
        compiler_params=pltpu.CompilerParams(
            collective_id=0, has_side_effects=True, vmem_limit_bytes=VMEM - 4 * CLASSES * (row_count + feat)
        ),
        name="tree",
    )(owners, features.reshape(n, seg, feat), ids, tags)

    planes, scores = pl.pallas_call(
        place_kernel,
        out_shape=(
            jax.ShapeDtypeStruct((CLASSES, feat), jnp.float32),
            jax.ShapeDtypeStruct((CLASSES, row_count), jnp.float32),
        ),
        in_specs=[whole, whole],
        out_specs=(hbm, hbm),
        scratch_shapes=[dma((2,))],
        name="place",
    )(*(pltpu.with_memory_space_constraint(x, pltpu.VMEM) for x in (planes, scores)))
    return planes[None], scores


def solution(mesh):
    in_specs = (P(("leaf", "rows"), None), P(("leaf", "rows")), P(("leaf", "rows")), P("leaf"))
    out_specs = (P(("leaf", "rows"), None, None), P(None, ("leaf", "rows")))
    return jax.shard_map(
        on_device, mesh=mesh, in_specs=in_specs, out_specs=out_specs, check_vma=False
    )
```
